256 devices in a mesh: group: 4 (over x), det: 8 (over z), tm: 8 (over y, core).
Axes of the slice: x: 4, y: 4, z: 8, core: 2. Of those that a mesh axis runs over, the one named last changes fastest.
Arguments:
- map_solution: float32 [3, 8, 256, 128], P(None, 'det', ('group', 'tm')), may hold values from -6 to 6
- map_residual: float32 [3, 8, 256, 128], P(None, 'det', ('group', 'tm')), may hold values from -6 to 6
- map_direction: float32 [3, 8, 256, 128], P(None, 'det', ('group', 'tm')), may hold values from -6 to 6
- hits: int32 [512, 1024], P(('group', 'det'), 'tm'), may hold values from 0 to 768, as said below
- stokes_int: int32 [2, 512, 131072], P(None, ('group', 'det'), 'tm'), may hold values from -2047 to 2047
- inv_noise: float32 [512, 512], P(('group', 'det')), may hold values from 0.2 to 2
Outputs:
- new_solution: float32 [3, 8, 256, 128], P(None, 'det', ('group', 'tm'))
- new_residual: float32 [3, 8, 256, 128], P(None, 'det', ('group', 'tm'))
- new_direction: float32 [3, 8, 256, 128], P(None, 'det', ('group', 'tm'))
The draws below stay inside these ranges and needn't reach their ends.
Inputs may be any that keep to these rules, and one draw needn't show every extreme that they name: `hits`: A value below 768 names a pixel block in the sky tile of the detector's det index or in one of its two neighbours along det, as the steps say; the value 768 marks a flagged block.
All inputs are finite; a program needn't handle non-finite values.
Results may differ from the reference program's by a relative error of at most 0.0003.
Values sent between devices are 32-bit elements; how exact they have to be, the bound alone decides.
A program may use at most 64 MiB of HBM per device.

```python
import math
import jax
import jax.numpy as jnp
from jax import lax

DET_DEV = 16
WIN = 1024
FREQS = 512
DETS = 512
SAMPLES = 131072
BLOCKS = 1024
TILES = 8
TILE_PB = 256
LOCAL = 768


def draw_hits(key, part):
    first_key, second_key = jax.random.split(jax.random.fold_in(key, 11))
    blocks = jax.random.randint(first_key, (DETS, BLOCKS), 0, LOCAL)
    flagged = jax.random.randint(second_key, (DETS, BLOCKS), 0, 8) == 0
    result = jnp.where(flagged, LOCAL, blocks)
    result = result.at[0, 0].set(LOCAL).at[0, 1].set(0)
    return result.astype(jnp.int32)


def set_ends(array, own_key, smallest, top_value):
    place = [jax.random.randint(jax.random.fold_in(own_key, axis), (), 0, length) for axis, length in enumerate(array.shape)]
    widest = array.shape.index(max(array.shape))
    next_to = place[:widest] + [(place[widest] + 1) % array.shape[widest]] + place[widest + 1:]
    return array.at[tuple(place)].set(smallest).at[tuple(next_to)].set(top_value)


def level_of(key, extent, shards, low, top_value):
    factor_of, own = 1.0, jax.random.fold_in(key, 6)
    for axis_at, parts in shards:
        draws = jnp.exp(jax.random.uniform(jax.random.fold_in(own, axis_at), (parts,), jnp.float32, low / len(shards), top_value / len(shards)))
        factor_of = factor_of * jnp.repeat(draws, extent[axis_at] // parts).reshape([-1 if axis == axis_at else 1 for axis in range(len(extent))])
    return factor_of


def scatter_about(stream_key, dims, width, reach, cuts=(), held_as=jnp.bfloat16):
    values = jax.random.normal(stream_key, dims, jnp.float32) * width
    if len(cuts) > 0:
        values = level_of(stream_key, dims, cuts, -0.22, 0.18) * values
    return jnp.clip(values, min=-reach, max=reach).astype(held_as)


def setup_inputs(seed: int = 0) -> dict:
    seeds = jax.random.split(jax.random.key(seed), 7)
    return {
        "map_solution": scatter_about(seeds[0], (3, TILES, TILE_PB, 128), 1.0, 6.0, ((1, 8), (2, 32)), jnp.float32),
        "map_residual": scatter_about(seeds[1], (3, TILES, TILE_PB, 128), 1.0, 6.0, ((1, 8), (2, 32)), jnp.float32),
        "map_direction": scatter_about(seeds[2], (3, TILES, TILE_PB, 128), 1.0, 6.0, ((1, 8), (2, 32)), jnp.float32),
        "hits": draw_hits(jax.random.fold_in(seeds[6], 71), 0),
        "stokes_int": set_ends(jax.random.randint(seeds[4], (2, DETS, SAMPLES), -2047, 2048), jax.random.fold_in(seeds[4], 1), -2047, 2047).astype(jnp.int32),
        "inv_noise": jnp.clip(jnp.exp(math.log(2.0) - 2.3025851 * jax.random.uniform(seeds[5], (DETS, FREQS), jnp.float32) ** level_of(seeds[5], (DETS, FREQS), ((0, 32),), -0.2, 0.2)), 0.2, 2.0),
    }


def basis_rows(length):
    row_ids = jnp.arange(length, dtype=jnp.int32)[:, None]
    sample_ids = jnp.arange(length, dtype=jnp.int32)[None, :]
    middle = length // 2
    frequency = jnp.where(row_ids <= middle, row_ids, row_ids - middle)
    phases = frequency * sample_ids % length
    angles = phases.astype(jnp.float32) * (2.0 * math.pi / length)
    values = jnp.where(row_ids > middle, jnp.sin(angles), jnp.cos(angles))
    scales = jnp.where((row_ids == 0) | (row_ids == middle), math.sqrt(1.0 / length), math.sqrt(2.0 / length))
    return values * scales

def noise_filter(extended, spectrum, basis_table):
    row_count = extended.shape[0]
    length = basis_table.shape[0]
    segment = length // 2
    pieces = extended.reshape(row_count, -1, segment)
    windows = jnp.concatenate([pieces[:, :-1], pieces[:, 1:]], axis=2)
    windows_count = windows.shape[1]
    weights = jnp.concatenate([spectrum, spectrum[:, -1:], spectrum[:, 1:]], axis=1)
    coeffs = jnp.dot(windows.reshape(-1, length), basis_table.T, precision=lax.Precision.HIGHEST)
    coeffs = coeffs.reshape(row_count, windows_count, length) * weights[:, None, :]
    restored = jnp.dot(coeffs.reshape(-1, length), basis_table, precision=lax.Precision.HIGHEST)
    restored = restored.reshape(row_count, windows_count, length)
    return (restored[:, :-1, segment:] + restored[:, 1:, :segment]).reshape(row_count, -1)

def reference(map_solution, map_residual, map_direction, hits, stokes_int, inv_noise):
    basis_table = basis_rows(WIN)
    segment = WIN // 2
    pixels = TILES * TILE_PB
    flat_direction = jnp.concatenate([map_direction.reshape(3, pixels, 128), jnp.zeros((3, 1, 128), jnp.float32)], axis=1)

    def one_block(binned, block_index):
        row_start = (block_index * DET_DEV).astype(jnp.int32)
        block_hits = lax.dynamic_slice_in_dim(hits, row_start, DET_DEV, 0)
        sky_tile = block_index % TILES
        tile_ids = (sky_tile + block_hits // TILE_PB - 1) % TILES
        indices = jnp.where(block_hits == LOCAL, pixels, tile_ids * TILE_PB + block_hits % TILE_PB).reshape(-1).astype(jnp.int32)
        weights_int = lax.dynamic_slice_in_dim(stokes_int, row_start, DET_DEV, 1)
        q_weight = (weights_int[0].astype(jnp.float32) / 2048.0).reshape(-1, 128)
        u_weight = (weights_int[1].astype(jnp.float32) / 2048.0).reshape(-1, 128)
        picked = jnp.take(flat_direction, indices, axis=1)
        scanned = (picked[0] + q_weight * picked[1] + u_weight * picked[2]).reshape(DET_DEV, SAMPLES)
        extended = jnp.pad(scanned, ((0, 0), (segment, segment)))
        spectrum = lax.dynamic_slice_in_dim(inv_noise, row_start, DET_DEV, 0)
        filtered = noise_filter(extended, spectrum, basis_table).reshape(-1, 128)
        block_terms = jnp.stack([jax.ops.segment_sum(values, indices, num_segments=pixels + 1) for values in (filtered, q_weight * filtered, u_weight * filtered)])
        return (binned + block_terms, None)
    binned, ignored = lax.scan(one_block, jnp.zeros((3, pixels + 1, 128), jnp.float32), jnp.arange(DETS // DET_DEV, dtype=jnp.int32))
    map_image = binned[:, :pixels].reshape(3, TILES, TILE_PB, 128)
    old_norm = jnp.sum(map_residual * map_residual)
    curvature = jnp.sum(map_direction * map_image)
    step_size = old_norm / curvature
    new_solution = map_solution + step_size * map_direction
    new_residual = map_residual - step_size * map_image
    new_norm = jnp.sum(new_residual * new_residual)
    new_direction = new_residual + new_norm / old_norm * map_direction
    return (new_solution, new_residual, new_direction)
```

```python
import math
import numpy as np
import jax, jax.numpy as jnp
from jax import lax
from jax.experimental import pallas as pl
from jax.experimental.pallas import tpu as pltpu
from jax.sharding import Mesh
from jax.sharding import PartitionSpec as P

BF = jnp.bfloat16
F32 = jnp.float32

def basis_tables():
    n = np.arange(256)[None, :]
    k = np.arange(256)[:, None]
    kk = np.where(k <= 128, k, k - 128)
    ang = 2 * np.pi * ((kk * n) % 256) / 256
    fe = np.where(k <= 128, np.cos(ang), np.sin(ang))
    fe = fe * np.where((k == 0) | (k == 128), math.sqrt(1 / 256), math.sqrt(2 / 256))
    kk = k % 128
    ang = 2 * np.pi * (((2 * kk + 1) * n) % 512) / 512
    fo = np.where(k < 128, np.cos(ang), np.sin(ang)) * math.sqrt(2 / 256)
    ang = 2 * np.pi * (((2 * k + 1) * n) % 1024) / 1024
    fc = np.cos(ang) / 16
    fs = np.sin(ang) / 16
    fs[:, 0] = np.where(np.arange(256) % 2 == 0, 1, -1) / 16
    return [fe, fo, fc, fs]

def split_np(a):
    a = np.asarray(a, np.float32)
    hi = a.astype(BF)
    lo = (a - hi.astype(np.float32)).astype(BF)
    return hi, lo

def tables():
    fe, fo, fc, fs = basis_tables()
    out = []
    for m in (fe.T, fo.T, fc.T, fs.T, fe * 0.5, fo * 0.5, fc, fs):
        hi, lo = split_np(m)
        out.append(np.concatenate([hi, lo], 0))
    return np.stack(out)

def split(x):
    hi = x.astype(BF)
    lo = (x - hi.astype(F32)).astype(BF)
    return hi, lo

def dot(a, b):
    return jnp.dot(a, b, preferred_element_type=F32)

def dot3(x, tab):
    hi, lo = split(x)
    th = tab[0:256, :]
    tl = tab[256:512, :]
    return dot(hi, th) + dot(hi, tl) + dot(lo, th)

def lane_iota(shape):
    return lax.broadcasted_iota(jnp.int32, shape, len(shape) - 1)

def take(x, idx):
    return jnp.take_along_axis(x, idx, axis=1)

def reverse256(a, b):
    lane = lane_iota(a.shape)
    p = lax.rem(128 - lane, 128)
    ap, bp = take(a, p), take(b, p)
    z = lane == 0
    return jnp.where(z, ap, bp), jnp.where(z, bp, ap)

def weight_tables(w):
    lane = lane_iota((16, 128))
    blk = [w[:, 128 * b:128 * b + 128] for b in range(4)]
    def pick(stride, off, blocks):
        per = 128 // stride
        idx = stride * lax.rem(lane, per) + off
        out = take(blk[blocks[0]], idx)
        for t, b in enumerate(blocks[1:], 1):
            out = jnp.where(lane // per == t, take(blk[b], idx), out)
        return out
    w0 = pick(4, 0, (0, 1, 2, 3))
    w2 = pick(4, 2, (0, 1, 2, 3))
    last = jnp.broadcast_to(w[:, 511:512], (16, 128))
    we = (w0, jnp.where(lane == 0, last, w0))
    wo = (w2, w2)
    wd = (pick(2, 1, (0, 1)), pick(2, 1, (2, 3)))
    return we, wo, wd

def hit_rows(hits):
    h = hits.astype(F32)
    a = jnp.floor(h * (1.0 / 256.0))
    b = h - 256.0 * a
    both = jnp.concatenate([a, b], 0).astype(BF)
    row = lax.broadcasted_iota(jnp.int32, (128, 2048), 0)
    col = lax.broadcasted_iota(jnp.int32, (128, 2048), 1)
    want = 4 * ((col // 16) % 32) + col // 512
    p = jnp.where(row == want, 1.0, 0.0).astype(BF)
    y = dot(both, p)
    y = 256.0 * y[:16] + y[16:]
    i = lax.broadcasted_iota(jnp.int32, (16, 2048), 0)
    c = lax.broadcasted_iota(jnp.int32, (16, 2048), 1)
    return jnp.sum(jnp.where(i == c % 16, y, 0.0), axis=0, keepdims=True)

def prepare(hits_ref, hh_ref, noise_ref, oh_ref, oht_ref, wt_ref):
    hits = hits_ref[...]
    halo = hh_ref[...]
    lane = lane_iota((16, 128))
    one = jnp.ones((16, 128), F32)
    zero = jnp.zeros((16, 128), F32)
    for s in range(34):
        for j in range(4):
            if s == 0:
                src = halo[:, j:j + 1]
            elif s == 33:
                src = halo[:, 4 + j:5 + j]
            else:
                c = 4 * (s - 1) + j
                src = hits[:, c:c + 1]
            hb = jnp.broadcast_to(src, (16, 128))
            for k in range(6):
                oh_ref[j, 16 * s:16 * s + 16, 128 * k:128 * k + 128] = jnp.where(
                    hb == lane + 128 * k, one, zero).astype(BF)
    hrow = hit_rows(hits)
    def rows(t, carry):
        base = pl.multiple_of(t * 16, 16)
        it = lax.broadcasted_iota(jnp.int32, (16, 2048), 0).astype(F32) + (t * 16).astype(F32)
        oht_ref[pl.ds(base, 16), :] = jnp.where(it == hrow, 1.0, 0.0).astype(BF)
        return carry
    lax.fori_loop(0, 48, rows, 0)
    we, wo, wd = weight_tables(noise_ref[...])
    for t, (a, b) in enumerate((we, wo, wd)):
        wt_ref[t, :, 0:128] = a
        wt_ref[t, :, 128:256] = b

def scan_samples(tab_ref, st_ref, sh_ref, oh_ref, x_ref):
    def one(j, carry):
        off = pl.multiple_of(j * 128, 128)
        g = dot(oh_ref[j], tab_ref[...])
        gi = g[:, 0:128] + g[:, 384:512]
        gq = g[:, 128:256] + g[:, 512:640]
        gu = g[:, 256:384] + g[:, 640:768]
        for s in range(34):
            r = slice(16 * s, 16 * s + 16)
            if s == 0 or s == 33:
                e = 0 if s == 0 else 1
                q = sh_ref[e, 0, :, pl.ds(off, 128)]
                u = sh_ref[e, 1, :, pl.ds(off, 128)]
            else:
                o = pl.multiple_of(off + 512 * (s - 1), 128)
                q = st_ref[0, :, pl.ds(o, 128)]
                u = st_ref[1, :, pl.ds(o, 128)]
            q = q.astype(F32) * (1.0 / 2048.0)
            u = u.astype(F32) * (1.0 / 2048.0)
            x_ref[r, pl.ds(off, 128)] = gi[r] + q * gq[r] + u * gu[r]
        return carry
    lax.fori_loop(0, 4, one, 0)

def noise_filter(x_ref, tb_ref, wt_ref, f_ref):
    M = 256
    def chunk(t, carry):
        base = pl.multiple_of(t * M, M)
        def xs(c, d):
            return x_ref[pl.ds(base + 16 * d, M), 128 * c:128 * c + 128]
        u, v = [], []
        for c in range(4):
            y = 0.5 * (xs(c, 0) + xs(c, 2))
            x = xs(c, 1)
            u.append(x + y)
            v.append(x - y)
        ue = jnp.concatenate([u[0] + u[2], u[1] + u[3]], 1)
        uo = jnp.concatenate([u[0] - u[2], u[1] - u[3]], 1)
        r0, r1 = reverse256(v[2], v[3])
        z = lane_iota((M, 128)) == 0
        vc = jnp.concatenate([v[0] - jnp.where(z, 0.0, r0), v[1] - r1], 1)
        vs = jnp.concatenate([jnp.where(z, r0, v[0] + r0), v[1] + r1], 1)
        outs = []
        for t_, (a, wi) in enumerate(((ue, 0), (uo, 1), (vc, 2), (vs, 2))):
            c = dot3(a, tb_ref[t_])
            c = (c.reshape(M // 16, 16, 256) * wt_ref[wi][None]).reshape(M, 256)
            outs.append(dot3(c, tb_ref[4 + t_]))
        ae, ao, oc, os_ = outs
        oc0, oc1, os0, os1 = oc[:, :128], oc[:, 128:], os_[:, :128], os_[:, 128:]
        p0, p1 = jnp.where(z, os0, os0 - oc0), os1 - oc1
        d2, d3 = reverse256(p0, p1)
        d0, d1 = oc0 + jnp.where(z, 0.0, os0), oc1 + os1
        ae0, ae1, ao0, ao1 = ae[:, :128], ae[:, 128:], ao[:, :128], ao[:, 128:]
        rows = pl.ds(base, M)
        f_ref[rows, 0:128] = ae0 + ao0 + d0
        f_ref[rows, 128:256] = ae1 + ao1 + d1
        f_ref[rows, 256:384] = ae0 - ao0 + d2
        f_ref[rows, 384:512] = ae1 - ao1 + d3
        return carry
    lax.fori_loop(0, 512 // M, chunk, 0)

def weighted(f_ref, st_ref, v_ref):
    def one(j, carry):
        off = pl.multiple_of(j * 128, 128)
        for s in range(32):
            r = slice(16 * s, 16 * s + 16)
            f = f_ref[r, pl.ds(off, 128)]
            o = pl.multiple_of(off + 512 * s, 128)
            q = st_ref[0, :, pl.ds(o, 128)].astype(F32) * (1.0 / 2048.0)
            u = st_ref[1, :, pl.ds(o, 128)].astype(F32) * (1.0 / 2048.0)
            vr = pl.ds(pl.multiple_of(j * 512 + 16 * s, 16), 16)
            for c, val in enumerate((f, q * f, u * f)):
                hi, lo = split(val)
                v_ref[vr, 128 * c:128 * c + 128] = hi
                v_ref[vr, 384 + 128 * c:512 + 128 * c] = lo
        return carry
    lax.fori_loop(0, 4, one, 0)

def bin_rows(oht_ref, v_ref, out_ref):
    M = 256
    def chunk(t, carry):
        rows = pl.ds(pl.multiple_of(t * M, M), M)
        g = dot(oht_ref[rows, :], v_ref[...])
        for c in range(3):
            out_ref[c, rows, :] = g[:, 128 * c:128 * c + 128] + g[:, 384 + 128 * c:512 + 128 * c]
        return carry
    lax.fori_loop(0, 768 // M, chunk, 0)

def kernel(win_ref, hits_ref, hh_ref, st_ref, sh_ref, noise_ref, tb_ref, out_ref,
           tab_ref, oh_ref, oht_ref, wt_ref, x_ref, f_ref, v_ref):
    prepare(hits_ref, hh_ref, noise_ref, oh_ref, oht_ref, wt_ref)
    for c in range(3):
        hi, lo = split(win_ref[c])
        tab_ref[:, 128 * c:128 * c + 128] = hi
        tab_ref[:, 384 + 128 * c:512 + 128 * c] = lo
    scan_samples(tab_ref, st_ref, sh_ref, oh_ref, x_ref)
    noise_filter(x_ref, tb_ref, wt_ref, f_ref)
    weighted(f_ref, st_ref, v_ref)
    bin_rows(oht_ref, v_ref, out_ref)

SCR = [
    pltpu.VMEM((768, 768), BF), pltpu.VMEM((4, 544, 768), BF), pltpu.VMEM((768, 2048), BF),
    pltpu.VMEM((3, 16, 256), F32), pltpu.VMEM((544, 512), F32), pltpu.VMEM((512, 512), F32),
    pltpu.VMEM((2048, 768), BF),
]
vm = pl.BlockSpec(memory_space=pltpu.VMEM)

def local(win, hits, hh, st, sh, noise, tb, kernel=kernel):
    return pl.pallas_call(
        kernel, out_shape=jax.ShapeDtypeStruct((3, 768, 128), F32),
        in_specs=[vm] * 7, out_specs=vm, scratch_shapes=SCR,
        compiler_params=pltpu.CompilerParams(vmem_limit_bytes=60 << 20),
    )(win, hits, hh, st, sh, noise, tb)


GROUP_TM = ("group", "tm_0", "tm_1")
TM = ("tm_0", "tm_1")
ALL = ("group", "det", "tm_0", "tm_1")


def from_everyone(value, axis):
    copies = jnp.broadcast_to(value, (lax.axis_size(axis), *value.shape))
    return lax.all_to_all(copies, axis, split_axis=0, concat_axis=0, tiled=True)


def shift(value, axis, by, periodic):
    n = lax.axis_size(axis)
    pairs = [(i, (i + by) % n) for i in range(n) if periodic or 0 <= i + by < n]
    return lax.ppermute(value, axis, pairs)


def shards(map_solution, map_residual, map_direction, hits, stokes_int, inv_noise):
    t = lax.axis_index(TM)
    lh = shift(hits[:, 124:], TM, 1, False)
    rh = shift(hits[:, :4], TM, -1, False)
    ls = shift(stokes_int[:, :, -512:], TM, 1, False)
    rs = shift(stokes_int[:, :, :512], TM, -1, False)
    lh = jnp.where(t == 0, 768, lh)
    rh = jnp.where(t == 7, 768, rh)
    hh = jnp.concatenate([lh, rh, jnp.zeros((16, 120), jnp.int32)], axis=1)
    sh = jnp.stack([ls, rs])
    tiles = from_everyone(map_direction[:, 0], GROUP_TM)
    tile = jnp.moveaxis(tiles, 0, 1).reshape(3, 256, 128)
    lower = shift(tile, "det", 1, True)
    upper = shift(tile, "det", -1, True)
    win = jnp.concatenate([lower, tile, upper], axis=1)
    binned = local(win, hits, hh, stokes_int, sh, inv_noise, jnp.asarray(tables()))
    parts = binned.reshape(3, 3, 32, 8, 128)
    parts = jnp.moveaxis(parts, 2, 0)
    got = lax.all_to_all(parts, GROUP_TM, split_axis=0, concat_axis=0, tiled=True).sum(axis=0)
    own = got[:, 1] + shift(got[:, 2], "det", 1, True) + shift(got[:, 0], "det", -1, True)
    map_image = own[:, None]
    sums = jnp.stack([
        jnp.sum(map_residual * map_residual),
        jnp.sum(map_direction * map_image),
        jnp.sum(map_residual * map_image),
        jnp.sum(map_image * map_image),
    ])
    for axis in ALL:
        sums = lax.psum(sums, axis)
    old_norm, curvature, cross_term, image_norm = sums[0], sums[1], sums[2], sums[3]
    step_size = old_norm / curvature
    new_residual = map_residual - step_size * map_image
    new_norm = old_norm - 2.0 * step_size * cross_term + step_size * step_size * image_norm
    new_solution = map_solution + step_size * map_direction
    new_direction = new_residual + new_norm / old_norm * map_direction
    return (new_solution, new_residual, new_direction)


def solution(mesh):
    torus = Mesh(
        mesh.devices.reshape(mesh.shape["group"], mesh.shape["det"], 4, 2),
        ("group", "det", "tm_0", "tm_1"),
    )
    tile = P(None, "det", GROUP_TM, None)
    in_specs = (tile, tile, tile, P(("group", "det"), TM), P(None, ("group", "det"), TM), P(("group", "det"), None))
    return jax.shard_map(shards, mesh=torus, in_specs=in_specs, out_specs=(tile, tile, tile), check_vma=False)
```

```python
import math
import numpy as np
import jax, jax.numpy as jnp
from jax import lax
from jax.experimental import pallas as pl
from jax.experimental.pallas import tpu as pltpu
from jax.sharding import Mesh
from jax.sharding import PartitionSpec as P

BF = jnp.bfloat16
F32 = jnp.float32

def basis_tables():
    n = np.arange(256)[None, :]
    k = np.arange(256)[:, None]
    kk = np.where(k <= 128, k, k - 128)
    ang = 2 * np.pi * ((kk * n) % 256) / 256
    fe = np.where(k <= 128, np.cos(ang), np.sin(ang))
    fe = fe * np.where((k == 0) | (k == 128), math.sqrt(1 / 256), math.sqrt(2 / 256))
    kk = k % 128
    ang = 2 * np.pi * (((2 * kk + 1) * n) % 512) / 512
    fo = np.where(k < 128, np.cos(ang), np.sin(ang)) * math.sqrt(2 / 256)
    ang = 2 * np.pi * (((2 * k + 1) * n) % 1024) / 1024
    fc = np.cos(ang) / 16
    fs = np.sin(ang) / 16
    fs[:, 0] = np.where(np.arange(256) % 2 == 0, 1, -1) / 16
    return [fe, fo, fc, fs]

def split_np(a):
    a = np.asarray(a, np.float32)
    hi = a.astype(BF)
    lo = (a - hi.astype(np.float32)).astype(BF)
    return hi, lo

def tables():
    fe, fo, fc, fs = basis_tables()
    out = []
    for m in (fe.T, fo.T, fc.T, fs.T, fe * 0.5, fo * 0.5, fc, fs):
        hi, lo = split_np(m)
        out.append(np.concatenate([hi, lo], 0))
    return np.stack(out)

def split(x):
    hi = x.astype(BF)
    lo = (x - hi.astype(F32)).astype(BF)
    return hi, lo

def dot(a, b):
    return jnp.dot(a, b, preferred_element_type=F32)

def dot3(x, tab):
    hi, lo = split(x)
    th = tab[0:256, :]
    tl = tab[256:512, :]
    return dot(hi, th) + dot(hi, tl) + dot(lo, th)

def lane_iota(shape):
    return lax.broadcasted_iota(jnp.int32, shape, len(shape) - 1)

def take(x, idx):
    return jnp.take_along_axis(x, idx, axis=1)

def reverse256(a, b):
    lane = lane_iota(a.shape)
    p = lax.rem(128 - lane, 128)
    ap, bp = take(a, p), take(b, p)
    z = lane == 0
    return jnp.where(z, ap, bp), jnp.where(z, bp, ap)

def weight_tables(w):
    lane = lane_iota((16, 128))
    blk = [w[:, 128 * b:128 * b + 128] for b in range(4)]
    def pick(stride, off, blocks):
        per = 128 // stride
        idx = stride * lax.rem(lane, per) + off
        out = take(blk[blocks[0]], idx)
        for t, b in enumerate(blocks[1:], 1):
            out = jnp.where(lane // per == t, take(blk[b], idx), out)
        return out
    w0 = pick(4, 0, (0, 1, 2, 3))
    w2 = pick(4, 2, (0, 1, 2, 3))
    last = jnp.broadcast_to(w[:, 511:512], (16, 128))
    we = (w0, jnp.where(lane == 0, last, w0))
    wo = (w2, w2)
    wd = (pick(2, 1, (0, 1)), pick(2, 1, (2, 3)))
    return we, wo, wd

def hit_rows(hits):
    h = hits.astype(F32)
    a = jnp.floor(h * (1.0 / 256.0))
    b = h - 256.0 * a
    both = jnp.concatenate([a, b], 0).astype(BF)
    row = lax.broadcasted_iota(jnp.int32, (128, 2048), 0)
    col = lax.broadcasted_iota(jnp.int32, (128, 2048), 1)
    want = 4 * ((col // 16) % 32) + col // 512
    p = jnp.where(row == want, 1.0, 0.0).astype(BF)
    y = dot(both, p)
    y = 256.0 * y[:16] + y[16:]
    i = lax.broadcasted_iota(jnp.int32, (16, 2048), 0)
    c = lax.broadcasted_iota(jnp.int32, (16, 2048), 1)
    return jnp.sum(jnp.where(i == c % 16, y, 0.0), axis=0, keepdims=True)

def one_hot_rows(oh_ref, hits, cols, s):
    lane = lane_iota((16, 128))
    for j in range(4):
        hb = jnp.broadcast_to(hits[:, cols + j:cols + j + 1], (16, 128))
        for k in range(6):
            oh_ref[j, 16 * s:16 * s + 16, 128 * k:128 * k + 128] = jnp.where(
                hb == lane + 128 * k, 1.0, 0.0).astype(BF)


def gather_side(hits_ref, oh_ref):
    hits = hits_ref[...]
    for s in range(32):
        one_hot_rows(oh_ref, hits, 4 * s, s + 1)


def bin_side(hits_ref, noise_ref, oht_ref, wt_ref):
    hits = hits_ref[...]
    hrow = hit_rows(hits)
    def rows(t, carry):
        base = pl.multiple_of(t * 16, 16)
        it = lax.broadcasted_iota(jnp.int32, (16, 2048), 0).astype(F32) + (t * 16).astype(F32)
        oht_ref[pl.ds(base, 16), :] = jnp.where(it == hrow, 1.0, 0.0).astype(BF)
        return carry
    lax.fori_loop(0, 48, rows, 0)
    we, wo, wd = weight_tables(noise_ref[...])
    for t, (a, b) in enumerate((we, wo, wd)):
        wt_ref[t, :, 0:128] = a
        wt_ref[t, :, 128:256] = b

def scan_samples(tab_ref, st_ref, sh_ref, oh_ref, x_ref):
    def one(j, carry):
        off = pl.multiple_of(j * 128, 128)
        g = dot(oh_ref[j], tab_ref[...])
        gi = g[:, 0:128] + g[:, 384:512]
        gq = g[:, 128:256] + g[:, 512:640]
        gu = g[:, 256:384] + g[:, 640:768]
        for s in range(34):
            r = slice(16 * s, 16 * s + 16)
            if s == 0 or s == 33:
                e = 0 if s == 0 else 1
                q = sh_ref[e, 0, :, pl.ds(off, 128)]
                u = sh_ref[e, 1, :, pl.ds(off, 128)]
            else:
                o = pl.multiple_of(off + 512 * (s - 1), 128)
                q = st_ref[0, :, pl.ds(o, 128)]
                u = st_ref[1, :, pl.ds(o, 128)]
            q = q.astype(F32) * (1.0 / 2048.0)
            u = u.astype(F32) * (1.0 / 2048.0)
            x_ref[r, pl.ds(off, 128)] = gi[r] + q * gq[r] + u * gu[r]
        return carry
    lax.fori_loop(0, 4, one, 0)

def noise_filter(x_ref, tb_ref, wt_ref, f_ref):
    M = 256
    def chunk(t, carry):
        base = pl.multiple_of(t * M, M)
        def xs(c, d):
            return x_ref[pl.ds(base + 16 * d, M), 128 * c:128 * c + 128]
        u, v = [], []
        for c in range(4):
            y = 0.5 * (xs(c, 0) + xs(c, 2))
            x = xs(c, 1)
            u.append(x + y)
            v.append(x - y)
        ue = jnp.concatenate([u[0] + u[2], u[1] + u[3]], 1)
        uo = jnp.concatenate([u[0] - u[2], u[1] - u[3]], 1)
        r0, r1 = reverse256(v[2], v[3])
        z = lane_iota((M, 128)) == 0
        vc = jnp.concatenate([v[0] - jnp.where(z, 0.0, r0), v[1] - r1], 1)
        vs = jnp.concatenate([jnp.where(z, r0, v[0] + r0), v[1] + r1], 1)
        outs = []
        for t_, (a, wi) in enumerate(((ue, 0), (uo, 1), (vc, 2), (vs, 2))):
            c = dot3(a, tb_ref[t_])
            c = (c.reshape(M // 16, 16, 256) * wt_ref[wi][None]).reshape(M, 256)
            outs.append(dot3(c, tb_ref[4 + t_]))
        ae, ao, oc, os_ = outs
        oc0, oc1, os0, os1 = oc[:, :128], oc[:, 128:], os_[:, :128], os_[:, 128:]
        p0, p1 = jnp.where(z, os0, os0 - oc0), os1 - oc1
        d2, d3 = reverse256(p0, p1)
        d0, d1 = oc0 + jnp.where(z, 0.0, os0), oc1 + os1
        ae0, ae1, ao0, ao1 = ae[:, :128], ae[:, 128:], ao[:, :128], ao[:, 128:]
        rows = pl.ds(base, M)
        f_ref[rows, 0:128] = ae0 + ao0 + d0
        f_ref[rows, 128:256] = ae1 + ao1 + d1
        f_ref[rows, 256:384] = ae0 - ao0 + d2
        f_ref[rows, 384:512] = ae1 - ao1 + d3
        return carry
    lax.fori_loop(0, 512 // M, chunk, 0)

def weighted(f_ref, st_ref, v_ref):
    def one(j, carry):
        off = pl.multiple_of(j * 128, 128)
        for s in range(32):
            r = slice(16 * s, 16 * s + 16)
            f = f_ref[r, pl.ds(off, 128)]
            o = pl.multiple_of(off + 512 * s, 128)
            q = st_ref[0, :, pl.ds(o, 128)].astype(F32) * (1.0 / 2048.0)
            u = st_ref[1, :, pl.ds(o, 128)].astype(F32) * (1.0 / 2048.0)
            vr = pl.ds(pl.multiple_of(j * 512 + 16 * s, 16), 16)
            for c, val in enumerate((f, q * f, u * f)):
                hi, lo = split(val)
                v_ref[vr, 128 * c:128 * c + 128] = hi
                v_ref[vr, 384 + 128 * c:512 + 128 * c] = lo
        return carry
    lax.fori_loop(0, 4, one, 0)

def bin_tile(t, oht_ref, v_ref, b_ref):
    g = dot(oht_ref[256 * t:256 * t + 256, :], v_ref[...])
    for c in range(3):
        v = g[:, 128 * c:128 * c + 128] + g[:, 384 + 128 * c:512 + 128 * c]
        for p in range(16):
            for k in range(2):
                b_ref[k, t, p, c] = v[16 * p + 8 * k:16 * p + 8 * k + 8]


MESH = pl.DeviceIdType.MESH
PLANE = [(dx, dy) for dx in (2, 1, 3, 0) for dy in (2, 1, 3, 0)]
NEAR = [(dx, dy, dz) for dz in (1, -1, 0) for dx, dy in PLANE]
COLUMN = [(dz, dc) for dz in (4, 3, 5, 2, 6, 1, 7, 0) for dc in (0, 1)]


def remote(src, dst, send, recv, where):
    return pltpu.make_async_remote_copy(
        src_ref=src, dst_ref=dst, send_sem=send, recv_sem=recv, device_id=where, device_id_type=MESH)


def kernel(sol_ref, res_ref, dir_ref, hits_ref, st_hbm, noise_ref, tb_hbm,
           nsol_ref, nres_ref, ndir_ref,
           w_ref, tab_ref, oh_ref, oht_ref, wt_ref, x_ref, f_ref, v_ref, b_ref, pr_ref, s_ref, r_ref,
           st_ref, tb_ref, sh_ref, hn_ref, n0_ref, n1_ref, m1_ref, n2_ref,
           st_sem, tb_sem, a_send, a_recv, ap_send, ap_recv, h_send, h_recv,
           c_send, c_recv, cp_send, cp_recv, n1_send, n1_recv, n2_send, n2_recv):
    g, d, ty, c = (lax.axis_index(a) for a in ("group", "det", "tm_0", "tm_1"))
    me = g * 4 + ty
    other = 1 - c
    partner = (g, d, ty, other)
    side = (g, d, lax.rem(ty + 3 + 2 * c, 4), other)

    def near(dx, dy, dz):
        return (lax.rem(g + dx, 4), lax.rem(d + dz + 8, 8), lax.rem(ty + dy, 4), c)

    def column(dz, dc):
        return (g, lax.rem(d + dz, 8), ty, c if dc == 0 else other)

    near_list = [near(*o) for o in NEAR if o != (0, 0, 0)]
    greet = near_list + [partner, side]
    greet += [column(dz, dc) for dz, dc in COLUMN if (dz, dc) != (0, 0) and (dz, dc) != (0, 1)
              and not (dc == 0 and dz in (1, 7))]
    barrier = pltpu.get_barrier_semaphore()
    for dev in greet:
        pl.semaphore_signal(barrier, inc=1, device_id=dev, device_id_type=MESH)
    load_st = pltpu.make_async_copy(st_hbm, st_ref, st_sem)
    load_tb = pltpu.make_async_copy(tb_hbm, tb_ref, tb_sem)
    load_st.start()
    load_tb.start()
    own = pltpu.make_async_copy(dir_ref, w_ref.at[c, 1, me], a_recv.at[1])
    own.start()
    bin_side(hits_ref, noise_ref, oht_ref, wt_ref)
    pl.semaphore_wait(barrier, len(greet))

    sends = []
    for k, o in enumerate(o for o in NEAR if o != (0, 0, 0)):
        sends.append(remote(dir_ref, w_ref.at[c, 1 - o[2], me], a_send.at[k], a_recv.at[1 - o[2]], near(*o)))
    load_st.wait()
    halo = []
    edge = 16384 - 512
    for k, (dev, off, slot) in enumerate(((partner, other * edge, c), (side, c * edge, other))):
        off = pl.multiple_of(off, 128)
        halo.append(remote(hits_ref, hn_ref.at[slot], h_send.at[2 * k], h_recv.at[slot], dev))
        halo.append(remote(st_ref.at[:, :, pl.ds(off, 512)], sh_ref.at[slot], h_send.at[2 * k + 1],
                           h_recv.at[2 + slot], dev))
    for copy in sends + halo:
        copy.start()
    gather_side(hits_ref, oh_ref)
    for k in range(2):
        remote(hits_ref, hn_ref.at[k], h_send.at[0], h_recv.at[k], partner).wait_recv()
        remote(sh_ref.at[k], sh_ref.at[k], h_send.at[0], h_recv.at[2 + k], partner).wait_recv()
    first = jnp.logical_and(ty == 0, c == 0)
    last = jnp.logical_and(ty == 3, c == 1)
    one_hot_rows(oh_ref, jnp.where(first, 768, hn_ref[0]), 124, 0)
    one_hot_rows(oh_ref, jnp.where(last, 768, hn_ref[1]), 0, 33)

    pairs = []
    for t in (0, 2, 1):
        pltpu.make_async_copy(w_ref.at[c, t], w_ref.at[c, t], a_recv.at[t]).wait()
        copy = remote(w_ref.at[c, t], w_ref.at[c, t], ap_send.at[t], ap_recv.at[t], partner)
        copy.start()
        pairs.append(copy)
    for t in (0, 2, 1):
        remote(w_ref.at[other, t], w_ref.at[other, t], ap_send.at[t], ap_recv.at[t], partner).wait_recv()
        def chip(p, carry):
            rows = pl.ds(pl.multiple_of(256 * t + 16 * p, 16), 16)
            for k in range(3):
                both = jnp.concatenate([w_ref[0, t, p, k], w_ref[1, t, p, k]], 0)
                hi, lo = split(both)
                tab_ref[rows, 128 * k:128 * k + 128] = hi
                tab_ref[rows, 384 + 128 * k:512 + 128 * k] = lo
            return carry
        lax.fori_loop(0, 16, chip, 0)
    scan_samples(tab_ref, st_ref, sh_ref, oh_ref, x_ref)
    load_tb.wait()
    noise_filter(x_ref, tb_ref, wt_ref, f_ref)
    weighted(f_ref, st_ref, v_ref)

    out_pairs = {}
    for t in (0, 2, 1):
        bin_tile(t, oht_ref, v_ref, b_ref)
        copy = remote(b_ref.at[other, t], pr_ref.at[t], cp_send.at[t], cp_recv.at[t], partner)
        copy.start()
        out_pairs[t] = copy
    outs = []
    for t in (0, 2, 1):
        out_pairs[t].wait_recv()
        s_ref[t] = b_ref[c, t] + pr_ref[t]
        for k, (dx, dy) in enumerate(PLANE):
            gx, yx = lax.rem(g + dx, 4), lax.rem(ty + dy, 4)
            src = s_ref.at[t, gx * 4 + yx]
            if (dx, dy, t) == (0, 0, 1):
                pltpu.make_async_copy(src, r_ref.at[t, me], c_recv).start()
                continue
            copy = remote(src, r_ref.at[t, me], c_send.at[16 * t + k], c_recv, near(dx, dy, t - 1))
            copy.start()
            outs.append(copy)
    pltpu.make_async_copy(r_ref, r_ref, c_recv).wait()
    image = r_ref[0, 0]
    for t in range(3):
        for p in range(16):
            if t + p:
                image = image + r_ref[t, p]
    res = res_ref[...]
    dire = dir_ref[...]

    def lanes(v):
        return jnp.sum(jnp.sum(v, axis=0), axis=0, keepdims=True)

    parts = [lanes(res * res), lanes(dire * image), lanes(res * image), lanes(image * image)]
    row = lax.broadcasted_iota(jnp.int32, (8, 128), 0)
    total = jnp.zeros((8, 128), F32)
    for k, p in enumerate(parts):
        total = jnp.where(row == k, jnp.broadcast_to(p, (8, 128)), total)
    n0_ref[...] = total
    norms = []
    pltpu.make_async_copy(n0_ref, n1_ref.at[me], n1_recv).start()
    for k, (dx, dy) in enumerate(PLANE):
        if (dx, dy) != (0, 0):
            norms.append(remote(n0_ref, n1_ref.at[me], n1_send.at[k], n1_recv, near(dx, dy, 0)))
            norms[-1].start()
    pltpu.make_async_copy(n1_ref, n1_ref, n1_recv).wait()
    m1_ref[...] = jnp.sum(n1_ref[...], axis=0)
    slot = d * 2 + c
    pltpu.make_async_copy(m1_ref, n2_ref.at[slot], n2_recv).start()
    for k, (dz, dc) in enumerate(COLUMN):
        if (dz, dc) != (0, 0):
            norms.append(remote(m1_ref, n2_ref.at[slot], n2_send.at[k], n2_recv, column(dz, dc)))
            norms[-1].start()
    pltpu.make_async_copy(n2_ref, n2_ref, n2_recv).wait()
    sums = jnp.sum(jnp.sum(n2_ref[...], axis=0), axis=1, keepdims=True)
    old_norm, curvature, cross_term, image_norm = (sums[k:k + 1] for k in range(4))
    step = old_norm / curvature
    new_norm = old_norm - 2.0 * step * cross_term + step * step * image_norm
    ratio = new_norm / old_norm
    for k in range(3):
        nsol_ref[k] = sol_ref[k] + step * dire[k]
        nr = res[k] - step * image[k]
        nres_ref[k] = nr
        ndir_ref[k] = nr + ratio * dire[k]
    for copy in sends + halo + pairs + list(out_pairs.values()) + outs + norms:
        copy.wait_send()


def step_kernel(sol, res, dire, hits, st, noise, tb):
    vm = pl.BlockSpec(memory_space=pltpu.VMEM)
    anyspace = pl.BlockSpec(memory_space=pl.ANY)
    shard = jax.ShapeDtypeStruct((3, 8, 128), F32)
    dma = pltpu.SemaphoreType.DMA
    scratch = [
        pltpu.VMEM((2, 3, 16, 3, 8, 128), F32), pltpu.VMEM((768, 768), BF), pltpu.VMEM((4, 544, 768), BF),
        pltpu.VMEM((768, 2048), BF), pltpu.VMEM((3, 16, 256), F32), pltpu.VMEM((544, 512), F32),
        pltpu.VMEM((512, 512), F32), pltpu.VMEM((2048, 768), BF), pltpu.VMEM((2, 3, 16, 3, 8, 128), F32),
        pltpu.VMEM((3, 16, 3, 8, 128), F32), pltpu.VMEM((3, 16, 3, 8, 128), F32),
        pltpu.VMEM((3, 16, 3, 8, 128), F32), pltpu.VMEM((2, 16, 16384), jnp.int32),
        pltpu.VMEM((8, 512, 256), BF), pltpu.VMEM((2, 2, 16, 512), jnp.int32), pltpu.VMEM((2, 16, 128), jnp.int32),
        pltpu.VMEM((8, 128), F32), pltpu.VMEM((16, 8, 128), F32), pltpu.VMEM((8, 128), F32),
        pltpu.VMEM((16, 8, 128), F32),
        dma, dma, dma((47,)), dma((3,)), dma((3,)), dma((3,)), dma((4,)), dma((4,)),
        dma((48,)), dma, dma((3,)), dma((3,)), dma((16,)), dma, dma((16,)), dma,
    ]
    return pl.pallas_call(
        kernel, out_shape=(shard, shard, shard),
        in_specs=[vm, vm, vm, vm, anyspace, vm, anyspace], out_specs=(vm, vm, vm), scratch_shapes=scratch,
        compiler_params=pltpu.CompilerParams(
            vmem_limit_bytes=60 << 20, collective_id=0, has_side_effects=True),
    )(sol, res, dire, hits, st, noise, tb)


def shards(map_solution, map_residual, map_direction, hits, stokes_int, inv_noise):
    outs = step_kernel(map_solution[:, 0], map_residual[:, 0], map_direction[:, 0], hits, stokes_int,
                       inv_noise, jnp.asarray(tables()))
    return tuple(o[:, None] for o in outs)


def solution(mesh):
    torus = Mesh(
        mesh.devices.reshape(mesh.shape["group"], mesh.shape["det"], 4, 2),
        ("group", "det", "tm_0", "tm_1"),
    )
    TM = ("tm_0", "tm_1")
    tile = P(None, "det", ("group",) + TM, None)
    in_specs = (tile, tile, tile, P(("group", "det"), TM), P(None, ("group", "det"), TM), P(("group", "det"), None))
    return jax.shard_map(shards, mesh=torus, in_specs=in_specs, out_specs=(tile, tile, tile), check_vma=False)
```

```python
import math
import numpy as np
import jax, jax.numpy as jnp
from jax import lax
from jax.experimental import pallas as pl
from jax.experimental.pallas import tpu as pltpu
from jax.sharding import Mesh
from jax.sharding import PartitionSpec as P

BF = jnp.bfloat16
F32 = jnp.float32

def basis_tables():
    n = np.arange(256)[None, :]
    k = np.arange(256)[:, None]
    kk = np.where(k <= 128, k, k - 128)
    ang = 2 * np.pi * ((kk * n) % 256) / 256
    fe = np.where(k <= 128, np.cos(ang), np.sin(ang))
    fe = fe * np.where((k == 0) | (k == 128), math.sqrt(1 / 256), math.sqrt(2 / 256))
    kk = k % 128
    ang = 2 * np.pi * (((2 * kk + 1) * n) % 512) / 512
    fo = np.where(k < 128, np.cos(ang), np.sin(ang)) * math.sqrt(2 / 256)
    ang = 2 * np.pi * (((2 * k + 1) * n) % 1024) / 1024
    fc = np.cos(ang) / 16
    fs = np.sin(ang) / 16
    fs[:, 0] = np.where(np.arange(256) % 2 == 0, 1, -1) / 16
    return [fe, fo, fc, fs]

def split_np(a):
    a = np.asarray(a, np.float32)
    hi = a.astype(BF)
    lo = (a - hi.astype(np.float32)).astype(BF)
    return hi, lo

def tables():
    fe, fo, fc, fs = basis_tables()
    out = []
    for m in (fe.T, fo.T, fc.T, fs.T, fe * 0.5, fo * 0.5, fc, fs):
        hi, lo = split_np(m)
        out.append(np.concatenate([hi, lo], 0))
    return np.stack(out)

def split(x):
    hi = x.astype(BF)
    lo = (x - hi.astype(F32)).astype(BF)
    return hi, lo

def dot(a, b):
    return jnp.dot(a, b, preferred_element_type=F32)

def dot3(x, tab):
    hi, lo = split(x)
    th = tab[0:256, :]
    tl = tab[256:512, :]
    return dot(hi, th) + dot(hi, tl) + dot(lo, th)

def lane_iota(shape):
    return lax.broadcasted_iota(jnp.int32, shape, len(shape) - 1)

def take(x, idx):
    return jnp.take_along_axis(x, idx, axis=1)

def reverse256(a, b):
    lane = lane_iota(a.shape)
    p = lax.rem(128 - lane, 128)
    ap, bp = take(a, p), take(b, p)
    z = lane == 0
    return jnp.where(z, ap, bp), jnp.where(z, bp, ap)

def weight_tables(w):
    lane = lane_iota((16, 128))
    blk = [w[:, 128 * b:128 * b + 128] for b in range(4)]
    def pick(stride, off, blocks):
        per = 128 // stride
        idx = stride * lax.rem(lane, per) + off
        out = take(blk[blocks[0]], idx)
        for t, b in enumerate(blocks[1:], 1):
            out = jnp.where(lane // per == t, take(blk[b], idx), out)
        return out
    w0 = pick(4, 0, (0, 1, 2, 3))
    w2 = pick(4, 2, (0, 1, 2, 3))
    last = jnp.broadcast_to(w[:, 511:512], (16, 128))
    we = (w0, jnp.where(lane == 0, last, w0))
    wo = (w2, w2)
    wd = (pick(2, 1, (0, 1)), pick(2, 1, (2, 3)))
    return we, wo, wd

def hit_rows(hits):
    h = hits.astype(F32)
    a = jnp.floor(h * (1.0 / 256.0))
    b = h - 256.0 * a
    both = jnp.concatenate([a, b], 0).astype(BF)
    row = lax.broadcasted_iota(jnp.int32, (128, 2048), 0)
    col = lax.broadcasted_iota(jnp.int32, (128, 2048), 1)
    want = 4 * ((col // 16) % 32) + col // 512
    p = jnp.where(row == want, 1.0, 0.0).astype(BF)
    y = dot(both, p)
    y = 256.0 * y[:16] + y[16:]
    i = lax.broadcasted_iota(jnp.int32, (16, 2048), 0)
    c = lax.broadcasted_iota(jnp.int32, (16, 2048), 1)
    return jnp.sum(jnp.where(i == c % 16, y, 0.0), axis=0, keepdims=True)

BASE = (256, 384, 0, 128, 512, 640)


def one_hot_rows(oh_ref, hits, cols, s):
    lane = lane_iota((16, 128))
    for j in range(4):
        hb = jnp.broadcast_to(hits[:, cols + j:cols + j + 1], (16, 128))
        for k in range(6):
            oh_ref[j, 16 * s:16 * s + 16, 128 * k:128 * k + 128] = jnp.where(
                hb == lane + BASE[k], 1.0, 0.0).astype(BF)


def gather_side(hits_ref, oh_ref):
    hits = hits_ref[...]
    for s in range(32):
        one_hot_rows(oh_ref, hits, 4 * s, s + 1)


def bin_side(hits_ref, noise_ref, oht_ref, wt_ref):
    hits = hits_ref[...]
    hrow = hit_rows(hits)
    def rows(t, carry):
        base = pl.multiple_of(t * 16, 16)
        it = lax.broadcasted_iota(jnp.int32, (16, 2048), 0).astype(F32) + (t * 16).astype(F32)
        oht_ref[pl.ds(base, 16), :] = jnp.where(it == hrow, 1.0, 0.0).astype(BF)
        return carry
    lax.fori_loop(0, 48, rows, 0)
    we, wo, wd = weight_tables(noise_ref[...])
    for t, (a, b) in enumerate((we, wo, wd)):
        wt_ref[t, :, 0:128] = a
        wt_ref[t, :, 128:256] = b

def scan_samples(lo, hi, tab_ref, st_ref, sh_ref, oh_ref, x_ref):
    def one(j, carry):
        off = pl.multiple_of(j * 128, 128)
        g = dot(oh_ref[j, :, lo:hi], tab_ref[lo:hi, :])
        gi = g[:, 0:128] + g[:, 384:512]
        gq = g[:, 128:256] + g[:, 512:640]
        gu = g[:, 256:384] + g[:, 640:768]
        for s in range(34):
            r = slice(16 * s, 16 * s + 16)
            if s == 0 or s == 33:
                e = 0 if s == 0 else 1
                q = sh_ref[e, 0, :, pl.ds(off, 128)]
                u = sh_ref[e, 1, :, pl.ds(off, 128)]
            else:
                o = pl.multiple_of(off + 512 * (s - 1), 128)
                q = st_ref[0, :, pl.ds(o, 128)]
                u = st_ref[1, :, pl.ds(o, 128)]
            q = q.astype(F32) * (1.0 / 2048.0)
            u = u.astype(F32) * (1.0 / 2048.0)
            v = gi[r] + q * gq[r] + u * gu[r]
            x_ref[r, pl.ds(off, 128)] = v if lo == 0 else x_ref[r, pl.ds(off, 128)] + v
        return carry
    lax.fori_loop(0, 4, one, 0)

def noise_filter(x_ref, tb_ref, wt_ref, f_ref):
    M = 256
    def chunk(t, carry):
        base = pl.multiple_of(t * M, M)
        def xs(c, d):
            return x_ref[pl.ds(base + 16 * d, M), 128 * c:128 * c + 128]
        u, v = [], []
        for c in range(4):
            y = 0.5 * (xs(c, 0) + xs(c, 2))
            x = xs(c, 1)
            u.append(x + y)
            v.append(x - y)
        ue = jnp.concatenate([u[0] + u[2], u[1] + u[3]], 1)
        uo = jnp.concatenate([u[0] - u[2], u[1] - u[3]], 1)
        r0, r1 = reverse256(v[2], v[3])
        z = lane_iota((M, 128)) == 0
        vc = jnp.concatenate([v[0] - jnp.where(z, 0.0, r0), v[1] - r1], 1)
        vs = jnp.concatenate([jnp.where(z, r0, v[0] + r0), v[1] + r1], 1)
        outs = []
        for t_, (a, wi) in enumerate(((ue, 0), (uo, 1), (vc, 2), (vs, 2))):
            c = dot3(a, tb_ref[t_])
            c = (c.reshape(M // 16, 16, 256) * wt_ref[wi][None]).reshape(M, 256)
            outs.append(dot3(c, tb_ref[4 + t_]))
        ae, ao, oc, os_ = outs
        oc0, oc1, os0, os1 = oc[:, :128], oc[:, 128:], os_[:, :128], os_[:, 128:]
        p0, p1 = jnp.where(z, os0, os0 - oc0), os1 - oc1
        d2, d3 = reverse256(p0, p1)
        d0, d1 = oc0 + jnp.where(z, 0.0, os0), oc1 + os1
        ae0, ae1, ao0, ao1 = ae[:, :128], ae[:, 128:], ao[:, :128], ao[:, 128:]
        rows = pl.ds(base, M)
        f_ref[rows, 0:128] = ae0 + ao0 + d0
        f_ref[rows, 128:256] = ae1 + ao1 + d1
        f_ref[rows, 256:384] = ae0 - ao0 + d2
        f_ref[rows, 384:512] = ae1 - ao1 + d3
        return carry
    lax.fori_loop(0, 512 // M, chunk, 0)

def weighted(f_ref, st_ref, v_ref):
    def one(j, carry):
        off = pl.multiple_of(j * 128, 128)
        for s in range(32):
            r = slice(16 * s, 16 * s + 16)
            f = f_ref[r, pl.ds(off, 128)]
            o = pl.multiple_of(off + 512 * s, 128)
            q = st_ref[0, :, pl.ds(o, 128)].astype(F32) * (1.0 / 2048.0)
            u = st_ref[1, :, pl.ds(o, 128)].astype(F32) * (1.0 / 2048.0)
            vr = pl.ds(pl.multiple_of(j * 512 + 16 * s, 16), 16)
            for c, val in enumerate((f, q * f, u * f)):
                hi, lo = split(val)
                v_ref[vr, 128 * c:128 * c + 128] = hi
                v_ref[vr, 384 + 128 * c:512 + 128 * c] = lo
        return carry
    lax.fori_loop(0, 4, one, 0)

def bin_tile(t, oht_ref, v_ref, b_ref):
    g = dot(oht_ref[256 * t:256 * t + 256, :], v_ref[...])
    for c in range(3):
        v = g[:, 128 * c:128 * c + 128] + g[:, 384 + 128 * c:512 + 128 * c]
        for p in range(16):
            for k in range(2):
                b_ref[k, t, p, c] = v[16 * p + 8 * k:16 * p + 8 * k + 8]


MESH = pl.DeviceIdType.MESH
PLANE = [(dx, dy) for dx in (2, 1, 3, 0) for dy in (2, 1, 3, 0)]
NEAR = [(dx, dy, dz) for dz in (0, 1, -1) for dx, dy in PLANE]
COLUMN = [(dz, dc) for dz in (4, 3, 5, 2, 6, 1, 7, 0) for dc in (0, 1)]


def remote(src, dst, send, recv, where):
    return pltpu.make_async_remote_copy(
        src_ref=src, dst_ref=dst, send_sem=send, recv_sem=recv, device_id=where, device_id_type=MESH)


def kernel(sol_hbm, res_hbm, dir_hbm, hits_hbm, st_hbm, noise_hbm, tb_hbm, out_ref,
           w_ref, tab_ref, oh_ref, oht_ref, wt_ref, x_ref, f_ref, v_ref, b_ref, pr_ref, s_ref, r_ref,
           st_ref, tb_ref, sh_ref, hn_ref, n0_ref, n1_ref, m1_ref, n2_ref, sol_ref, res_ref, dir_ref, hits_ref, noise_ref,
           in_sem, a_send, a_recv, ap_send, ap_recv, h_send, h_recv,
           c_send, c_recv, cp_send, cp_recv, n1_send, n1_recv, n2_send, n2_recv):
    g, d, ty, c = (lax.axis_index(a) for a in ("group", "det", "tm_0", "tm_1"))
    me = g * 4 + ty
    other = 1 - c
    partner = (g, d, ty, other)
    side = (g, d, lax.rem(ty + 3 + 2 * c, 4), other)

    def near(dx, dy, dz):
        return (lax.rem(g + dx, 4), lax.rem(d + dz + 8, 8), lax.rem(ty + dy, 4), c)

    def column(dz, dc):
        return (g, lax.rem(d + dz, 8), ty, c if dc == 0 else other)

    near_list = [near(*o) for o in NEAR if o != (0, 0, 0)]
    greet = near_list + [partner, side]
    greet += [column(dz, dc) for dz, dc in COLUMN if (dz, dc) != (0, 0) and (dz, dc) != (0, 1)
              and not (dc == 0 and dz in (1, 7))]
    barrier = pltpu.get_barrier_semaphore()
    for dev in greet:
        pl.semaphore_signal(barrier, inc=1, device_id=dev, device_id_type=MESH)
    own = pltpu.make_async_copy(dir_hbm, w_ref.at[c, 1, me], a_recv.at[1])
    own.start()
    loads = [pltpu.make_async_copy(src, dst, in_sem.at[k]) for k, (src, dst) in enumerate((
        (hits_hbm, hits_ref), (noise_hbm, noise_ref), (st_hbm, st_ref), (tb_hbm, tb_ref),
        (res_hbm, res_ref), (dir_hbm, dir_ref), (sol_hbm, sol_ref)))]
    for copy in loads:
        copy.start()
    load_hits, load_noise, load_st, load_tb, load_res, load_dir, load_sol = loads
    pl.semaphore_wait(barrier, len(greet))

    halo = []
    edge = 16384 - 512
    for k, (dev, off, slot) in enumerate(((partner, other * edge, c), (side, c * edge, other))):
        off = pl.multiple_of(off, 128)
        halo.append(remote(hits_hbm, hn_ref.at[slot], h_send.at[2 * k], h_recv.at[slot], dev))
        halo.append(remote(st_hbm.at[:, :, pl.ds(off, 512)], sh_ref.at[slot], h_send.at[2 * k + 1],
                           h_recv.at[2 + slot], dev))
    for copy in halo:
        copy.start()
    sends = []
    for o in (o for o in NEAR if o != (0, 0, 0)):
        sends.append(remote(dir_hbm, w_ref.at[c, 1 - o[2], me], a_send, a_recv.at[1 - o[2]], near(*o)))
        sends[-1].start()
    load_hits.wait()
    load_noise.wait()
    gather_side(hits_ref, oh_ref)
    bin_side(hits_ref, noise_ref, oht_ref, wt_ref)
    load_st.wait()
    for k in range(2):
        remote(hits_hbm, hn_ref.at[k], h_send.at[0], h_recv.at[k], partner).wait_recv()
        remote(sh_ref.at[k], sh_ref.at[k], h_send.at[0], h_recv.at[2 + k], partner).wait_recv()
    first = jnp.logical_and(ty == 0, c == 0)
    last = jnp.logical_and(ty == 3, c == 1)
    one_hot_rows(oh_ref, jnp.where(first, 768, hn_ref[0]), 124, 0)
    one_hot_rows(oh_ref, jnp.where(last, 768, hn_ref[1]), 0, 33)

    pairs = []

    def swap(t):
        pltpu.make_async_copy(w_ref.at[c, t], w_ref.at[c, t], a_recv.at[t]).wait()
        copy = remote(w_ref.at[c, t], w_ref.at[c, t], ap_send.at[t], ap_recv.at[t], partner)
        copy.start()
        pairs.append(copy)

    def fill(t):
        remote(w_ref.at[other, t], w_ref.at[other, t], ap_send.at[t], ap_recv.at[t], partner).wait_recv()
        base = (256, 0, 512)[t]

        def chip(p, carry):
            rows = pl.ds(pl.multiple_of(base + 16 * p, 16), 16)
            for k in range(3):
                both = jnp.concatenate([w_ref[0, t, p, k], w_ref[1, t, p, k]], 0)
                hi, lo = split(both)
                tab_ref[rows, 128 * k:128 * k + 128] = hi
                tab_ref[rows, 384 + 128 * k:512 + 128 * k] = lo
            return carry
        lax.fori_loop(0, 16, chip, 0)

    swap(1)
    fill(1)
    scan_samples(0, 256, tab_ref, st_ref, sh_ref, oh_ref, x_ref)
    swap(0)
    swap(2)
    fill(0)
    fill(2)
    scan_samples(256, 768, tab_ref, st_ref, sh_ref, oh_ref, x_ref)
    load_tb.wait()
    noise_filter(x_ref, tb_ref, wt_ref, f_ref)
    weighted(f_ref, st_ref, v_ref)

    out_pairs = {}
    outs = []

    def bin_and_swap(t):
        bin_tile(t, oht_ref, v_ref, b_ref)
        out_pairs[t] = remote(b_ref.at[other, t], pr_ref.at[t], cp_send.at[t], cp_recv.at[t], partner)
        out_pairs[t].start()

    def send_tile(t):
        out_pairs[t].wait_recv()
        s_ref[t] = b_ref[c, t] + pr_ref[t]
        for k, (dx, dy) in enumerate(PLANE):
            gx, yx = lax.rem(g + dx, 4), lax.rem(ty + dy, 4)
            src = s_ref.at[t, gx * 4 + yx]
            if (dx, dy, t) == (0, 0, 1):
                pltpu.make_async_copy(src, r_ref.at[16 * t + me], c_recv).start()
                continue
            copy = remote(src, r_ref.at[16 * t + me], c_send, c_recv, near(dx, dy, t - 1))
            copy.start()
            outs.append(copy)

    bin_and_swap(0)
    bin_and_swap(2)
    send_tile(0)
    bin_and_swap(1)
    send_tile(2)
    send_tile(1)
    load_res.wait()
    load_dir.wait()
    load_sol.wait()
    pltpu.make_async_copy(r_ref, r_ref, c_recv).wait()
    image = r_ref[0]
    for p in range(1, 48):
        image = image + r_ref[p]
    res = res_ref[...]
    dire = dir_ref[...]

    def lanes(v):
        return jnp.sum(jnp.sum(v, axis=0), axis=0, keepdims=True)

    parts = [lanes(res * res), lanes(dire * image), lanes(res * image), lanes(image * image)]
    row = lax.broadcasted_iota(jnp.int32, (8, 128), 0)
    total = jnp.zeros((8, 128), F32)
    for k, p in enumerate(parts):
        total = jnp.where(row == k, jnp.broadcast_to(p, (8, 128)), total)
    n0_ref[...] = total
    norms = []
    pltpu.make_async_copy(n0_ref, n1_ref.at[me], n1_recv).start()
    for k, (dx, dy) in enumerate(PLANE):
        if (dx, dy) != (0, 0):
            norms.append(remote(n0_ref, n1_ref.at[me], n1_send, n1_recv, near(dx, dy, 0)))
            norms[-1].start()
    pltpu.make_async_copy(n1_ref, n1_ref, n1_recv).wait()
    m1_ref[...] = jnp.sum(n1_ref[...], axis=0)
    slot = d * 2 + c
    pltpu.make_async_copy(m1_ref, n2_ref.at[slot], n2_recv).start()
    for k, (dz, dc) in enumerate(COLUMN):
        if (dz, dc) != (0, 0):
            norms.append(remote(m1_ref, n2_ref.at[slot], n2_send, n2_recv, column(dz, dc)))
            norms[-1].start()
    for copy in halo + pairs + list(out_pairs.values()):
        copy.wait_send()
    pltpu.make_async_copy(r_ref.at[0:47], r_ref.at[0:47], a_send).wait()
    pltpu.make_async_copy(r_ref.at[0:47], r_ref.at[0:47], c_send).wait()
    pltpu.make_async_copy(n2_ref, n2_ref, n2_recv).wait()
    sums = jnp.sum(jnp.sum(n2_ref[...], axis=0), axis=1, keepdims=True)
    old_norm, curvature, cross_term, image_norm = (sums[k:k + 1] for k in range(4))
    step = old_norm / curvature
    new_norm = old_norm - 2.0 * step * cross_term + step * step * image_norm
    ratio = new_norm / old_norm
    for k in range(3):
        out_ref[0, k] = sol_ref[k] + step * dire[k]
        nr = res[k] - step * image[k]
        out_ref[1, k] = nr
        out_ref[2, k] = nr + ratio * dire[k]
    pltpu.make_async_copy(n1_ref.at[0:15], n1_ref.at[0:15], n1_send).wait()
    pltpu.make_async_copy(n1_ref.at[0:15], n1_ref.at[0:15], n2_send).wait()


def step_kernel(sol, res, dire, hits, st, noise, tb):
    hbm = pl.BlockSpec(memory_space=pltpu.HBM)
    dma = pltpu.SemaphoreType.DMA
    scratch = [
        pltpu.VMEM((2, 3, 16, 3, 8, 128), F32), pltpu.VMEM((768, 768), BF), pltpu.VMEM((4, 544, 768), BF),
        pltpu.VMEM((768, 2048), BF), pltpu.VMEM((3, 16, 256), F32), pltpu.VMEM((544, 512), F32),
        pltpu.VMEM((512, 512), F32), pltpu.VMEM((2048, 768), BF), pltpu.VMEM((2, 3, 16, 3, 8, 128), F32),
        pltpu.VMEM((3, 16, 3, 8, 128), F32), pltpu.VMEM((3, 16, 3, 8, 128), F32),
        pltpu.VMEM((48, 3, 8, 128), F32), pltpu.VMEM((2, 16, 16384), jnp.int32),
        pltpu.VMEM((8, 512, 256), BF), pltpu.VMEM((2, 2, 16, 512), jnp.int32), pltpu.VMEM((2, 16, 128), jnp.int32),
        pltpu.VMEM((8, 128), F32), pltpu.VMEM((16, 8, 128), F32), pltpu.VMEM((8, 128), F32),
        pltpu.VMEM((16, 8, 128), F32), pltpu.VMEM((3, 8, 128), F32), pltpu.VMEM((3, 8, 128), F32),
        pltpu.VMEM((3, 8, 128), F32),
        pltpu.VMEM((16, 128), jnp.int32), pltpu.VMEM((16, 512), F32),
        dma((7,)), dma, dma((3,)), dma((3,)), dma((3,)), dma((4,)), dma((4,)),
        dma, dma, dma((3,)), dma((3,)), dma, dma, dma, dma,
    ]
    return pl.pallas_call(
        kernel, out_shape=jax.ShapeDtypeStruct((3, 3, 8, 128), F32),
        in_specs=[hbm] * 7, out_specs=pl.BlockSpec(memory_space=pltpu.VMEM), scratch_shapes=scratch,
        compiler_params=pltpu.CompilerParams(
            vmem_limit_bytes=40 << 20, collective_id=0, has_side_effects=True),
    )(*(pltpu.with_memory_space_constraint(a, pltpu.HBM) for a in (sol, res, dire, hits, st, noise, tb)))


def shards(map_solution, map_residual, map_direction, hits, stokes_int, inv_noise):
    out = step_kernel(map_solution[:, 0], map_residual[:, 0], map_direction[:, 0], hits, stokes_int, inv_noise,
                      jnp.asarray(tables()))
    return (out[0][:, None], out[1][:, None], out[2][:, None])


def solution(mesh):
    torus = Mesh(
        mesh.devices.reshape(mesh.shape["group"], mesh.shape["det"], 4, 2),
        ("group", "det", "tm_0", "tm_1"),
    )
    TM = ("tm_0", "tm_1")
    tile = P(None, "det", ("group",) + TM, None)
    in_specs = (tile, tile, tile, P(("group", "det"), TM), P(None, ("group", "det"), TM), P(("group", "det"), None))
    return jax.shard_map(shards, mesh=torus, in_specs=in_specs, out_specs=(tile, tile, tile), check_vma=False)
```

```python
import math
import numpy as np
import jax, jax.numpy as jnp
from jax import lax
from jax.experimental import pallas as pl
from jax.experimental.pallas import tpu as pltpu
from jax.sharding import Mesh
from jax.sharding import PartitionSpec as P

BF = jnp.bfloat16
F32 = jnp.float32

def basis_tables():
    n = np.arange(256)[None, :]
    k = np.arange(256)[:, None]
    kk = np.where(k <= 128, k, k - 128)
    ang = 2 * np.pi * ((kk * n) % 256) / 256
    fe = np.where(k <= 128, np.cos(ang), np.sin(ang))
    fe = fe * np.where((k == 0) | (k == 128), math.sqrt(1 / 256), math.sqrt(2 / 256))
    kk = k % 128
    ang = 2 * np.pi * (((2 * kk + 1) * n) % 512) / 512
    fo = np.where(k < 128, np.cos(ang), np.sin(ang)) * math.sqrt(2 / 256)
    ang = 2 * np.pi * (((2 * k + 1) * n) % 1024) / 1024
    fc = np.cos(ang) / 16
    fs = np.sin(ang) / 16
    fs[:, 0] = np.where(np.arange(256) % 2 == 0, 1, -1) / 16
    return [fe, fo, fc, fs]

def split_np(a):
    a = np.asarray(a, np.float32)
    hi = a.astype(BF)
    lo = (a - hi.astype(np.float32)).astype(BF)
    return hi, lo

def tables():
    fe, fo, fc, fs = basis_tables()
    out = []
    for m in (fe.T, fo.T, fc.T, fs.T, fe * 0.5, fo * 0.5, fc, fs):
        hi, lo = split_np(m)
        out.append(np.concatenate([hi, lo], 0))
    return np.stack(out)

def split(x):
    hi = x.astype(BF)
    lo = (x - hi.astype(F32)).astype(BF)
    return hi, lo

def dot(a, b):
    return jnp.dot(a, b, preferred_element_type=F32)

def dot3(x, tab):
    hi, lo = split(x)
    th = tab[0:256, :]
    tl = tab[256:512, :]
    return dot(hi, th) + dot(hi, tl) + dot(lo, th)

def lane_iota(shape):
    return lax.broadcasted_iota(jnp.int32, shape, len(shape) - 1)

def take(x, idx):
    return jnp.take_along_axis(x, idx, axis=1)

def reverse256(a, b):
    lane = lane_iota(a.shape)
    p = lax.rem(128 - lane, 128)
    ap, bp = take(a, p), take(b, p)
    z = lane == 0
    return jnp.where(z, ap, bp), jnp.where(z, bp, ap)

def weight_tables(w):
    lane = lane_iota((16, 128))
    blk = [w[:, 128 * b:128 * b + 128] for b in range(4)]
    def pick(stride, off, blocks):
        per = 128 // stride
        idx = stride * lax.rem(lane, per) + off
        out = take(blk[blocks[0]], idx)
        for t, b in enumerate(blocks[1:], 1):
            out = jnp.where(lane // per == t, take(blk[b], idx), out)
        return out
    w0 = pick(4, 0, (0, 1, 2, 3))
    w2 = pick(4, 2, (0, 1, 2, 3))
    last = jnp.broadcast_to(w[:, 511:512], (16, 128))
    we = (w0, jnp.where(lane == 0, last, w0))
    wo = (w2, w2)
    wd = (pick(2, 1, (0, 1)), pick(2, 1, (2, 3)))
    return we, wo, wd

def hit_rows(hits):
    h = hits.astype(F32)
    a = jnp.floor(h * (1.0 / 256.0))
    b = h - 256.0 * a
    both = jnp.concatenate([a, b], 0).astype(BF)
    row = lax.broadcasted_iota(jnp.int32, (128, 2048), 0)
    col = lax.broadcasted_iota(jnp.int32, (128, 2048), 1)
    want = 4 * ((col // 16) % 32) + col // 512
    p = jnp.where(row == want, 1.0, 0.0).astype(BF)
    y = dot(both, p)
    y = 256.0 * y[:16] + y[16:]
    i = lax.broadcasted_iota(jnp.int32, (16, 2048), 0)
    c = lax.broadcasted_iota(jnp.int32, (16, 2048), 1)
    return jnp.sum(jnp.where(i == c % 16, y, 0.0), axis=0, keepdims=True)

BASE = (256, 384, 0, 128, 512, 640)


def one_hot_rows(oh_ref, hits, cols, s):
    lane = lane_iota((16, 128))
    for j in range(4):
        hb = jnp.broadcast_to(hits[:, cols + j:cols + j + 1], (16, 128))
        for k in range(6):
            oh_ref[j, 16 * s:16 * s + 16, 128 * k:128 * k + 128] = jnp.where(
                hb == lane + BASE[k], 1.0, 0.0).astype(BF)


def gather_side(hits_ref, oh_ref):
    hits = hits_ref[...]
    for s in range(32):
        one_hot_rows(oh_ref, hits, 4 * s, s + 1)


def bin_side(hits_ref, noise_ref, oht_ref, wt_ref):
    hits = hits_ref[...]
    hrow = hit_rows(hits)
    def rows(t, carry):
        base = pl.multiple_of(t * 16, 16)
        it = lax.broadcasted_iota(jnp.int32, (16, 2048), 0).astype(F32) + (t * 16).astype(F32)
        oht_ref[pl.ds(base, 16), :] = jnp.where(it == hrow, 1.0, 0.0).astype(BF)
        return carry
    lax.fori_loop(0, 48, rows, 0)
    we, wo, wd = weight_tables(noise_ref[...])
    for t, (a, b) in enumerate((we, wo, wd)):
        wt_ref[t, :, 0:128] = a
        wt_ref[t, :, 128:256] = b

def scan_samples(lo, hi, tab_ref, st_ref, sh_ref, oh_ref, x_ref):
    def one(j, carry):
        off = j * 128
        g = dot(oh_ref[j, :, lo:hi], tab_ref[lo:hi, :])
        gi = g[:, 0:128] + g[:, 384:512]
        gq = g[:, 128:256] + g[:, 512:640]
        gu = g[:, 256:384] + g[:, 640:768]
        for s in range(34):
            r = slice(16 * s, 16 * s + 16)
            if s == 0 or s == 33:
                e = 0 if s == 0 else 1
                q = sh_ref[e, 0, :, pl.ds(off, 128)]
                u = sh_ref[e, 1, :, pl.ds(off, 128)]
            else:
                o = off + 512 * (s - 1)
                q = st_ref[0, :, pl.ds(o, 128)]
                u = st_ref[1, :, pl.ds(o, 128)]
            q = q.astype(F32) * (1.0 / 2048.0)
            u = u.astype(F32) * (1.0 / 2048.0)
            v = gi[r] + q * gq[r] + u * gu[r]
            x_ref[r, pl.ds(off, 128)] = v if lo == 0 else x_ref[r, pl.ds(off, 128)] + v
        return carry
    for j in range(4):
        one(j, 0)

def noise_filter(x_ref, tb_ref, wt_ref, st_ref, v_ref):
    M = 512
    def chunk(t, carry):
        base = t * M
        def xs(c, d):
            return x_ref[pl.ds(base + 16 * d, M), 128 * c:128 * c + 128]
        u, v = [], []
        for c in range(4):
            y = 0.5 * (xs(c, 0) + xs(c, 2))
            x = xs(c, 1)
            u.append(x + y)
            v.append(x - y)
        ue = jnp.concatenate([u[0] + u[2], u[1] + u[3]], 1)
        uo = jnp.concatenate([u[0] - u[2], u[1] - u[3]], 1)
        r0, r1 = reverse256(v[2], v[3])
        z = lane_iota((M, 128)) == 0
        vc = jnp.concatenate([v[0] - jnp.where(z, 0.0, r0), v[1] - r1], 1)
        vs = jnp.concatenate([jnp.where(z, r0, v[0] + r0), v[1] + r1], 1)
        outs = []
        for t_, (a, wi) in enumerate(((ue, 0), (uo, 1), (vc, 2), (vs, 2))):
            c = dot3(a, tb_ref[t_])
            c = (c.reshape(M // 16, 16, 256) * wt_ref[wi][None]).reshape(M, 256)
            outs.append(dot3(c, tb_ref[4 + t_]))
        ae, ao, oc, os_ = outs
        oc0, oc1, os0, os1 = oc[:, :128], oc[:, 128:], os_[:, :128], os_[:, 128:]
        p0, p1 = jnp.where(z, os0, os0 - oc0), os1 - oc1
        d2, d3 = reverse256(p0, p1)
        d0, d1 = oc0 + jnp.where(z, 0.0, os0), oc1 + os1
        ae0, ae1, ao0, ao1 = ae[:, :128], ae[:, 128:], ao[:, :128], ao[:, 128:]
        for j, f in enumerate((ae0 + ao0 + d0, ae1 + ao1 + d1, ae0 - ao0 + d2, ae1 - ao1 + d3)):
            for i in range(M // 16):
                s = t * (M // 16) + i
                o = 128 * j + 512 * s
                q = st_ref[0, :, o:o + 128].astype(F32) * (1.0 / 2048.0)
                w = st_ref[1, :, o:o + 128].astype(F32) * (1.0 / 2048.0)
                r = 512 * j + 16 * s
                fi = f[16 * i:16 * i + 16]
                for k, val in enumerate((fi, q * fi, w * fi)):
                    hi, lo = split(val)
                    v_ref[r:r + 16, 256 * k:256 * k + 128] = hi
                    v_ref[r:r + 16, 256 * k + 128:256 * k + 256] = lo
        return carry
    for t in range(512 // M):
        chunk(t, 0)


def bin_map(c, oht_ref, v_ref, b_ref):
    g = jnp.concatenate([dot(oht_ref[384 * h:384 * h + 384, :], v_ref[:, 256 * c:256 * c + 256]) for h in range(2)], 0)
    v = g[:, 0:128] + g[:, 128:256]
    for p in range(48):
        x, y = p % 16 // 4, p % 4
        b_ref[0, c, y, p // 16, x] = v[16 * p:16 * p + 8]
        b_ref[1, c, x, p // 16, y] = v[16 * p + 8:16 * p + 16]


MESH = pl.DeviceIdType.MESH
NEAR = [(k, dz) for k in (2, 1, 3, 0) for dz in (1, -1, 0) if (k, dz) != (0, 0)]
RELAY = [(1, 0), (3, 0), (2, 0), (0, 1), (0, -1), (1, 1), (1, -1), (3, 1), (3, -1), (2, 1), (2, -1)]


def remote(src, dst, send, recv, where):
    return pltpu.make_async_remote_copy(
        src_ref=src, dst_ref=dst, send_sem=send, recv_sem=recv, device_id=where, device_id_type=MESH)


def kernel(sol_hbm, res_hbm, dir_hbm, hits_hbm, st_hbm, noise_hbm, tb_hbm, out_ref,
           w_ref, tab_ref, oh_ref, oht_ref, wt_ref, x_ref, v_ref, b_ref, pr_ref, s_ref, q_ref, t_ref, r_ref,
           st_ref, tb_ref, sh_ref, hn_ref, n0_ref, n1_ref, m1_ref, n2_ref, sol_ref, res_ref, dir_ref, hits_ref,
           noise_ref, in_sem, own_sem, a_send, a_recv, s2_recv, ap_send, ap_recv, h_send, h_recv,
           q_send, q_recv, c_send, c_recv, cp_send, cp_recv, n1_send, n1_recv, n2_send, n2_recv):
    g, d, ty, c = (lax.axis_index(a) for a in ("group", "det", "tm_0", "tm_1"))
    other = 1 - c
    a = g * other + ty * c
    b = ty * other + g * c
    me = 4 * b + a
    partner = (g, d, ty, other)
    side = (g, d, lax.rem(ty + 3 + 2 * c, 4), other)

    def at(k, m, dz):
        pa, pb = lax.rem(a + k, 4), lax.rem(b + m, 4)
        return (pa * other + pb * c, lax.rem(d + dz + 8, 8), pb * other + pa * c, c)

    greet = [at(k, 0, dz) for k, dz in NEAR] + [at(0, m, 0) for m in (2, 1, 3)] + [at(0, 0, 4), side, partner]
    barrier = pltpu.get_barrier_semaphore()
    for dev in greet:
        pl.semaphore_signal(barrier, inc=1, device_id=dev, device_id_type=MESH)
    own = pltpu.make_async_copy(dir_hbm, w_ref.at[c, 16 + me], own_sem)
    own.start()
    loads = [pltpu.make_async_copy(src, dst, in_sem.at[k]) for k, (src, dst) in enumerate((
        (hits_hbm, hits_ref), (noise_hbm, noise_ref), (st_hbm, st_ref), (tb_hbm, tb_ref),
        (res_hbm, res_ref), (dir_hbm, dir_ref), (sol_hbm, sol_ref)))]
    for copy in loads:
        copy.start()
    load_hits, load_noise, load_st, load_tb, load_res, load_dir, load_sol = loads
    pl.semaphore_wait(barrier, len(greet))

    for k, dz in NEAR:
        remote(dir_hbm, w_ref.at[c, 16 * (1 - dz) + me], a_send, a_recv.at[3 * k + dz + 1], at(k, 0, dz)).start()
    for m in (2, 1, 3):
        remote(dir_hbm, w_ref.at[c, 16 + me], a_send, s2_recv.at[1], at(0, m, 0)).start()
    halo = []
    edge = 16384 - 512
    for k, (dev, off, slot) in enumerate(((partner, other * edge, c), (side, c * edge, other))):
        off = pl.multiple_of(off, 128)
        halo.append(remote(hits_hbm, hn_ref.at[slot], h_send.at[2 * k], h_recv.at[slot], dev))
        halo.append(remote(st_hbm.at[:, :, pl.ds(off, 512)], sh_ref.at[slot], h_send.at[2 * k + 1],
                           h_recv.at[2 + slot], dev))
    for copy in halo:
        copy.start()

    def relay(k, dz):
        shard = w_ref.at[c, 16 * (1 - dz) + 4 * b + lax.rem(a + 4 - k, 4)]
        remote(shard, shard, a_send, a_recv.at[3 * k + dz + 1], partner).wait_recv()
        for m in (2, 1, 3):
            remote(shard, shard, a_send, s2_recv.at[1 - dz], at(0, m, 0)).start()

    load_hits.wait()
    gather_side(hits_ref, oh_ref)
    for k, dz in RELAY[:3]:
        relay(k, dz)
    for k, dz in RELAY[3:]:
        relay(k, dz)
    load_noise.wait()
    bin_side(hits_ref, noise_ref, oht_ref, wt_ref)
    load_st.wait()
    own.wait()
    for k in range(2):
        remote(hits_hbm, hn_ref.at[k], h_send.at[0], h_recv.at[k], partner).wait_recv()
        remote(sh_ref.at[k], sh_ref.at[k], h_send.at[0], h_recv.at[2 + k], partner).wait_recv()
    first = jnp.logical_and(ty == 0, c == 0)
    last = jnp.logical_and(ty == 3, c == 1)
    one_hot_rows(oh_ref, jnp.where(first, 768, hn_ref[0]), 124, 0)
    one_hot_rows(oh_ref, jnp.where(last, 768, hn_ref[1]), 0, 33)

    pairs = []

    def swap(t):
        pltpu.make_async_copy(w_ref.at[c, 16 * t:16 * t + 12], w_ref.at[c, 16 * t:16 * t + 12], s2_recv.at[t]).wait()
        copy = remote(w_ref.at[c, 16 * t:16 * t + 16], w_ref.at[c, 16 * t:16 * t + 16], ap_send.at[t], ap_recv.at[t], partner)
        copy.start()
        pairs.append(copy)

    def fill(t):
        remote(w_ref.at[other, 16 * t:16 * t + 16], w_ref.at[other, 16 * t:16 * t + 16], ap_send.at[t], ap_recv.at[t], partner).wait_recv()
        base = (256, 0, 512)[t]

        def chip(p, carry):
            rows = pl.ds(pl.multiple_of(base + 16 * p, 16), 16)
            for k in range(3):
                both = jnp.concatenate([w_ref[0, 16 * t + 4 * lax.rem(p, 4) + p // 4, k], w_ref[1, 16 * t + p, k]], 0)
                hi, lo = split(both)
                tab_ref[rows, 128 * k:128 * k + 128] = hi
                tab_ref[rows, 384 + 128 * k:512 + 128 * k] = lo
            return carry
        lax.fori_loop(0, 16, chip, 0)

    swap(1)
    swap(0)
    swap(2)
    fill(1)
    scan_samples(0, 256, tab_ref, st_ref, sh_ref, oh_ref, x_ref)
    fill(0)
    fill(2)
    scan_samples(256, 768, tab_ref, st_ref, sh_ref, oh_ref, x_ref)
    load_tb.wait()
    noise_filter(x_ref, tb_ref, wt_ref, st_ref, v_ref)

    out_pairs = []

    def bin_and_swap(k):
        bin_map(k, oht_ref, v_ref, b_ref)
        out_pairs.append(remote(b_ref.at[other, k], pr_ref.at[k], cp_send.at[k], cp_recv.at[k], partner))
        out_pairs[k].start()

    def send_map(k):
        out_pairs[k].wait_recv()
        s_ref[k] = b_ref[c, k] + pr_ref[k]
        for m in (2, 1, 3):
            remote(s_ref.at[k, lax.rem(b + m, 4)], q_ref.at[k, m - 1], q_send, q_recv.at[k], at(0, m, 0)).start()

    def pass_map(k):
        pltpu.make_async_copy(q_ref.at[k], q_ref.at[k], q_recv.at[k]).wait()
        t_ref[k] = s_ref[k, b] + q_ref[k, 0] + q_ref[k, 1] + q_ref[k, 2]
        for t in (0, 2, 1):
            for n in (2, 1, 3, 0):
                src = t_ref.at[k, t, lax.rem(a + n, 4)]
                dst = r_ref.at[12 * k + 4 * t + a]
                if (n, t) == (0, 1):
                    pltpu.make_async_copy(src, dst, c_recv.at[k]).start()
                else:
                    remote(src, dst, c_send, c_recv.at[k], at(n, 0, t - 1)).start()

    bin_and_swap(0)
    bin_and_swap(1)
    send_map(0)
    bin_and_swap(2)
    send_map(1)
    send_map(2)
    pass_map(0)
    pass_map(1)
    pass_map(2)
    load_res.wait()
    load_dir.wait()
    load_sol.wait()
    image = []
    parts = [jnp.zeros((8, 128), F32)] * 4
    for k in range(3):
        pltpu.make_async_copy(r_ref.at[12 * k:12 * k + 12], r_ref.at[12 * k:12 * k + 12], c_recv.at[k]).wait()
        m = r_ref[12 * k]
        for p in range(1, 12):
            m = m + r_ref[12 * k + p]
        image.append(m)
        res, dire = res_ref[k], dir_ref[k]
        parts = [p + v for p, v in zip(parts, (res * res, dire * m, res * m, m * m))]
    parts = [jnp.sum(p, axis=0, keepdims=True) for p in parts]
    part = lane_iota((1, 128)) // 32
    total = jnp.zeros((1, 128), F32)
    for k, p in enumerate(parts):
        p = p + pltpu.roll(p, 64, 1)
        p = p + pltpu.roll(p, 32, 1)
        total = jnp.where(part == k, p, total)
    n0_ref[...] = total
    cell = 8 * g + 2 * ty + c
    pltpu.make_async_copy(n0_ref, n1_ref.at[cell], n1_recv).start()
    for dx in (2, 1, 3, 0):
        for dy in (2, 1, 3, 0):
            for core in (other, c) if dx + dy else (other,):
                dev = (lax.rem(g + dx, 4), d, lax.rem(ty + dy, 4), core)
                remote(n0_ref, n1_ref.at[cell], n1_send, n1_recv, dev).start()
    pltpu.make_async_copy(n1_ref, n1_ref, n1_recv).wait()
    m1_ref[...] = jnp.sum(n1_ref[...], axis=0)
    pltpu.make_async_copy(m1_ref, n2_ref.at[d], n2_recv).start()
    for dz in (4, 3, 5, 2, 6, 1, 7):
        remote(m1_ref, n2_ref.at[d], n2_send, n2_recv, at(0, 0, dz)).start()
    for copy in halo + pairs + out_pairs:
        copy.wait_send()
    pltpu.make_async_copy(w_ref.at[0, 0:47], w_ref.at[0, 0:47], a_send).wait()
    pltpu.make_async_copy(q_ref, q_ref, q_send).wait()
    pltpu.make_async_copy(r_ref.at[0:33], r_ref.at[0:33], c_send).wait()
    pltpu.make_async_copy(n2_ref, n2_ref, n2_recv).wait()
    sums = jnp.sum(n2_ref[...], axis=0)
    old_norm, curvature, cross_term, image_norm = (
        jnp.sum(jnp.where(part == k, sums, 0.0), axis=1, keepdims=True) for k in range(4))
    step = old_norm / curvature
    new_norm = old_norm - 2.0 * step * cross_term + step * step * image_norm
    ratio = new_norm / old_norm
    for k in range(3):
        dire = dir_ref[k]
        out_ref[0, k] = sol_ref[k] + step * dire
        nr = res_ref[k] - step * image[k]
        out_ref[1, k] = nr
        out_ref[2, k] = nr + ratio * dire
    pltpu.make_async_copy(n1_ref.at[0:31], n1_ref.at[0:31], n1_send).wait()
    pltpu.make_async_copy(n2_ref.at[0:7], n2_ref.at[0:7], n2_send).wait()


def step_kernel(sol, res, dire, hits, st, noise, tb):
    hbm = pl.BlockSpec(memory_space=pltpu.HBM)
    dma = pltpu.SemaphoreType.DMA
    scratch = [
        pltpu.VMEM((2, 48, 3, 8, 128), F32), pltpu.VMEM((768, 768), BF), pltpu.VMEM((4, 544, 768), BF),
        pltpu.VMEM((768, 2048), BF), pltpu.VMEM((3, 16, 256), F32), pltpu.VMEM((544, 512), F32),
        pltpu.VMEM((2048, 768), BF), pltpu.VMEM((2, 3, 4, 3, 4, 8, 128), F32),
        pltpu.VMEM((3, 4, 3, 4, 8, 128), F32), pltpu.VMEM((3, 4, 3, 4, 8, 128), F32),
        pltpu.VMEM((3, 3, 3, 4, 8, 128), F32), pltpu.VMEM((3, 3, 4, 8, 128), F32), pltpu.VMEM((36, 8, 128), F32),
        pltpu.VMEM((2, 16, 16384), jnp.int32), pltpu.VMEM((8, 512, 256), BF),
        pltpu.VMEM((2, 2, 16, 512), jnp.int32), pltpu.VMEM((2, 16, 128), jnp.int32),
        pltpu.VMEM((1, 128), F32), pltpu.VMEM((32, 1, 128), F32), pltpu.VMEM((1, 128), F32),
        pltpu.VMEM((8, 1, 128), F32), pltpu.VMEM((3, 8, 128), F32), pltpu.VMEM((3, 8, 128), F32),
        pltpu.VMEM((3, 8, 128), F32), pltpu.VMEM((16, 128), jnp.int32), pltpu.VMEM((16, 512), F32),
        dma((7,)), dma, dma, dma((12,)), dma((3,)), dma((3,)), dma((3,)), dma((4,)), dma((4,)),
        dma, dma((3,)), dma, dma((3,)), dma((3,)), dma((3,)), dma, dma, dma, dma,
    ]
    return pl.pallas_call(
        kernel, out_shape=jax.ShapeDtypeStruct((3, 3, 8, 128), F32),
        in_specs=[hbm] * 7, out_specs=pl.BlockSpec(memory_space=pltpu.VMEM), scratch_shapes=scratch,
        compiler_params=pltpu.CompilerParams(
            vmem_limit_bytes=40 << 20, collective_id=0, has_side_effects=True),
    )(*(pltpu.with_memory_space_constraint(a, pltpu.HBM) for a in (sol, res, dire, hits, st, noise, tb)))


def shards(map_solution, map_residual, map_direction, hits, stokes_int, inv_noise):
    out = step_kernel(map_solution[:, 0], map_residual[:, 0], map_direction[:, 0], hits, stokes_int, inv_noise,
                      jnp.asarray(tables()))
    return (out[0][:, None], out[1][:, None], out[2][:, None])


def solution(mesh):
    torus = Mesh(
        mesh.devices.reshape(mesh.shape["group"], mesh.shape["det"], 4, 2),
        ("group", "det", "tm_0", "tm_1"),
    )
    TM = ("tm_0", "tm_1")
    tile = P(None, "det", ("group",) + TM, None)
    in_specs = (tile, tile, tile, P(("group", "det"), TM), P(None, ("group", "det"), TM), P(("group", "det"), None))
    return jax.shard_map(shards, mesh=torus, in_specs=in_specs, out_specs=(tile, tile, tile), check_vma=False)
```

```python
import math
import numpy as np
import jax, jax.numpy as jnp
from jax import lax
from jax.experimental import pallas as pl
from jax.experimental.pallas import tpu as pltpu
from jax.sharding import Mesh
from jax.sharding import PartitionSpec as P

BF = jnp.bfloat16
F32 = jnp.float32

def basis_tables():
    n = np.arange(256)[None, :]
    k = np.arange(256)[:, None]
    kk = np.where(k <= 128, k, k - 128)
    ang = 2 * np.pi * ((kk * n) % 256) / 256
    fe = np.where(k <= 128, np.cos(ang), np.sin(ang))
    fe = fe * np.where((k == 0) | (k == 128), math.sqrt(1 / 256), math.sqrt(2 / 256))
    kk = k % 128
    ang = 2 * np.pi * (((2 * kk + 1) * n) % 512) / 512
    fo = np.where(k < 128, np.cos(ang), np.sin(ang)) * math.sqrt(2 / 256)
    ang = 2 * np.pi * (((2 * k + 1) * n) % 1024) / 1024
    fc = np.cos(ang) / 16
    fs = np.sin(ang) / 16
    fs[:, 0] = np.where(np.arange(256) % 2 == 0, 1, -1) / 16
    return [fe, fo, fc, fs]

def split_np(a):
    a = np.asarray(a, np.float32)
    hi = a.astype(BF)
    lo = (a - hi.astype(np.float32)).astype(BF)
    return hi, lo

def tables():
    fe, fo, fc, fs = basis_tables()
    out = []
    for m in (fe.T, fo.T, fc.T, fs.T, fe * 0.5, fo * 0.5, fc, fs):
        hi, lo = split_np(m)
        out.append(np.concatenate([hi, lo], 0))
    return np.stack(out)

def split(x):
    hi = x.astype(BF)
    lo = (x - hi.astype(F32)).astype(BF)
    return hi, lo

def dot(a, b):
    return jnp.dot(a, b, preferred_element_type=F32)

def dot3(x, tab):
    hi, lo = split(x)
    th = tab[0:256, :]
    tl = tab[256:512, :]
    return dot(hi, th) + dot(hi, tl) + dot(lo, th)

def lane_iota(shape):
    return lax.broadcasted_iota(jnp.int32, shape, len(shape) - 1)

def take(x, idx):
    return jnp.take_along_axis(x, idx, axis=1)

def reverse256(a, b):
    lane = lane_iota(a.shape)
    p = lax.rem(128 - lane, 128)
    ap, bp = take(a, p), take(b, p)
    z = lane == 0
    return jnp.where(z, ap, bp), jnp.where(z, bp, ap)

def weight_tables(w):
    lane = lane_iota((16, 128))
    blk = [w[:, 128 * b:128 * b + 128] for b in range(4)]
    def pick(stride, off, blocks):
        per = 128 // stride
        idx = stride * lax.rem(lane, per) + off
        out = take(blk[blocks[0]], idx)
        for t, b in enumerate(blocks[1:], 1):
            out = jnp.where(lane // per == t, take(blk[b], idx), out)
        return out
    w0 = pick(4, 0, (0, 1, 2, 3))
    w2 = pick(4, 2, (0, 1, 2, 3))
    last = jnp.broadcast_to(w[:, 511:512], (16, 128))
    we = (w0, jnp.where(lane == 0, last, w0))
    wo = (w2, w2)
    wd = (pick(2, 1, (0, 1)), pick(2, 1, (2, 3)))
    return we, wo, wd

def hit_rows(hits):
    h = hits.astype(F32)
    a = jnp.floor(h * (1.0 / 256.0))
    b = h - 256.0 * a
    both = jnp.concatenate([a, b], 0).astype(BF)
    row = lax.broadcasted_iota(jnp.int32, (128, 2048), 0)
    col = lax.broadcasted_iota(jnp.int32, (128, 2048), 1)
    want = 4 * ((col // 16) % 32) + col // 512
    p = jnp.where(row == want, 1.0, 0.0).astype(BF)
    y = dot(both, p)
    y = 256.0 * y[:16] + y[16:]
    i = lax.broadcasted_iota(jnp.int32, (16, 2048), 0)
    c = lax.broadcasted_iota(jnp.int32, (16, 2048), 1)
    return jnp.sum(jnp.where(i == c % 16, y, 0.0), axis=0, keepdims=True)

def block_ids(tile, core):
    lane = lane_iota((16, 128))
    place, row = lane // 8, lax.rem(lane, 8)
    chip = (1 - core) * (4 * lax.rem(place, 4) + place // 4) + core * place
    return 256 * tile + 16 * chip + 8 * core + row


def halves(core):
    return [block_ids(t, k) for t, k in ((1, core), (1, 1 - core), (0, core), (2, core), (0, 1 - core), (2, 1 - core))]


def one_hot_rows(oh_ref, hits, cols, s, ids):
    for j in range(4):
        hb = jnp.broadcast_to(hits[:, cols + j:cols + j + 1], (16, 128))
        for k in range(6):
            oh_ref[j, 16 * s:16 * s + 16, 128 * k:128 * k + 128] = jnp.where(hb == ids[k], 1.0, 0.0).astype(BF)


def gather_side(hits_ref, oh_ref, ids):
    hits = hits_ref[...]
    for s in range(32):
        one_hot_rows(oh_ref, hits, 4 * s, s + 1, ids)


def bin_side(hits_ref, noise_ref, oht_ref, wt_ref):
    hits = hits_ref[...]
    hrow = hit_rows(hits)
    def rows(t, carry):
        base = pl.multiple_of(t * 16, 16)
        it = lax.broadcasted_iota(jnp.int32, (16, 2048), 0).astype(F32) + (t * 16).astype(F32)
        oht_ref[pl.ds(base, 16), :] = jnp.where(it == hrow, 1.0, 0.0).astype(BF)
        return carry
    lax.fori_loop(0, 48, rows, 0)
    we, wo, wd = weight_tables(noise_ref[...])
    for t, (a, b) in enumerate((we, wo, wd)):
        wt_ref[t, :, 0:128] = a
        wt_ref[t, :, 128:256] = b

def scan_samples(lo, hi, tab_ref, st_ref, sh_ref, oh_ref, x_ref):
    def one(j, carry):
        off = j * 128
        g = dot(oh_ref[j, :, lo:hi], tab_ref[lo:hi, :])
        gi = g[:, 0:128] + g[:, 384:512]
        gq = g[:, 128:256] + g[:, 512:640]
        gu = g[:, 256:384] + g[:, 640:768]
        for s in range(34):
            r = slice(16 * s, 16 * s + 16)
            if s == 0 or s == 33:
                e = 0 if s == 0 else 1
                q = sh_ref[e, 0, :, pl.ds(off, 128)]
                u = sh_ref[e, 1, :, pl.ds(off, 128)]
            else:
                o = off + 512 * (s - 1)
                q = st_ref[0, :, pl.ds(o, 128)]
                u = st_ref[1, :, pl.ds(o, 128)]
            q = q.astype(F32) * (1.0 / 2048.0)
            u = u.astype(F32) * (1.0 / 2048.0)
            v = gi[r] + q * gq[r] + u * gu[r]
            x_ref[r, pl.ds(off, 128)] = v if lo == 0 else x_ref[r, pl.ds(off, 128)] + v
        return carry
    for j in range(4):
        one(j, 0)

def noise_filter(x_ref, tb_ref, wt_ref, st_ref, v_ref):
    M = 512
    def chunk(t, carry):
        base = t * M
        def xs(c, d):
            return x_ref[pl.ds(base + 16 * d, M), 128 * c:128 * c + 128]
        u, v = [], []
        for c in range(4):
            y = 0.5 * (xs(c, 0) + xs(c, 2))
            x = xs(c, 1)
            u.append(x + y)
            v.append(x - y)
        ue = jnp.concatenate([u[0] + u[2], u[1] + u[3]], 1)
        uo = jnp.concatenate([u[0] - u[2], u[1] - u[3]], 1)
        r0, r1 = reverse256(v[2], v[3])
        z = lane_iota((M, 128)) == 0
        vc = jnp.concatenate([v[0] - jnp.where(z, 0.0, r0), v[1] - r1], 1)
        vs = jnp.concatenate([jnp.where(z, r0, v[0] + r0), v[1] + r1], 1)
        outs = []
        for t_, (a, wi) in enumerate(((ue, 0), (uo, 1), (vc, 2), (vs, 2))):
            c = dot3(a, tb_ref[t_])
            c = (c.reshape(M // 16, 16, 256) * wt_ref[wi][None]).reshape(M, 256)
            outs.append(dot3(c, tb_ref[4 + t_]))
        ae, ao, oc, os_ = outs
        oc0, oc1, os0, os1 = oc[:, :128], oc[:, 128:], os_[:, :128], os_[:, 128:]
        p0, p1 = jnp.where(z, os0, os0 - oc0), os1 - oc1
        d2, d3 = reverse256(p0, p1)
        d0, d1 = oc0 + jnp.where(z, 0.0, os0), oc1 + os1
        ae0, ae1, ao0, ao1 = ae[:, :128], ae[:, 128:], ao[:, :128], ao[:, 128:]
        for j, f in enumerate((ae0 + ao0 + d0, ae1 + ao1 + d1, ae0 - ao0 + d2, ae1 - ao1 + d3)):
            for i in range(M // 16):
                s = t * (M // 16) + i
                o = 128 * j + 512 * s
                q = st_ref[0, :, o:o + 128].astype(F32) * (1.0 / 2048.0)
                w = st_ref[1, :, o:o + 128].astype(F32) * (1.0 / 2048.0)
                r = 512 * j + 16 * s
                fi = f[16 * i:16 * i + 16]
                for k, val in enumerate((fi, q * fi, w * fi)):
                    hi, lo = split(val)
                    v_ref[r:r + 16, 256 * k:256 * k + 128] = hi
                    v_ref[r:r + 16, 256 * k + 128:256 * k + 256] = lo
        return carry
    for t in range(512 // M):
        chunk(t, 0)


def bin_map(c, oht_ref, v_ref, b_ref):
    g = jnp.concatenate([dot(oht_ref[384 * h:384 * h + 384, :], v_ref[:, 256 * c:256 * c + 256]) for h in range(2)], 0)
    v = g[:, 0:128] + g[:, 128:256]
    for p in range(48):
        x, y = p % 16 // 4, p % 4
        b_ref[0, c, y, p // 16, x] = v[16 * p:16 * p + 8]
        b_ref[1, c, x, p // 16, y] = v[16 * p + 8:16 * p + 16]


MESH = pl.DeviceIdType.MESH
NEAR = [(k, dz) for k in (2, 1, 3, 0) for dz in (1, -1, 0) if (k, dz) != (0, 0)]
RELAY = [(1, 0), (3, 0), (2, 0), (0, 1), (0, -1), (1, 1), (1, -1), (3, 1), (3, -1), (2, 1), (2, -1)]


def remote(src, dst, send, recv, where):
    return pltpu.make_async_remote_copy(
        src_ref=src, dst_ref=dst, send_sem=send, recv_sem=recv, device_id=where, device_id_type=MESH)


def kernel(sol_hbm, res_hbm, dir_hbm, hits_hbm, st_hbm, noise_hbm, tb_hbm, out_ref,
           w_ref, tab_ref, oh_ref, oht_ref, wt_ref, x_ref, v_ref, b_ref, pr_ref, s_ref, q_ref, t_ref, r_ref,
           st_ref, tb_ref, sh_ref, hn_ref, n0_ref, n1_ref, m1_ref, n2_ref, sol_ref, res_ref, dir_ref, hits_ref,
           noise_ref, in_sem, own_sem, a_send, a_recv, s2_recv, ap_send, ap_recv, h_send, h_recv,
           q_send, q_recv, c_send, c_recv, cp_send, cp_recv, n1_send, n1_recv, n2_send, n2_recv, hand_sem):
    g, d, ty, c = (lax.axis_index(a) for a in ("group", "det", "tm_0", "tm_1"))
    other = 1 - c
    a = g * other + ty * c
    b = ty * other + g * c
    me = 4 * b + a
    partner = (g, d, ty, other)
    side = (g, d, lax.rem(ty + 3 + 2 * c, 4), other)

    def at(k, m, dz):
        pa, pb = lax.rem(a + k, 4), lax.rem(b + m, 4)
        return (pa * other + pb * c, lax.rem(d + dz + 8, 8), pb * other + pa * c, c)

    greet = [at(k, 0, dz) for k, dz in NEAR] + [at(0, m, 0) for m in (2, 1, 3)] + [side, partner]
    barrier = pltpu.get_barrier_semaphore()
    for dev in greet:
        pl.semaphore_signal(barrier, inc=1, device_id=dev, device_id_type=MESH)
    own = pltpu.make_async_copy(dir_hbm, w_ref.at[c, 16 + me], own_sem)
    own.start()
    loads = [pltpu.make_async_copy(src, dst, in_sem.at[k]) for k, (src, dst) in enumerate((
        (hits_hbm, hits_ref), (noise_hbm, noise_ref), (st_hbm, st_ref), (tb_hbm, tb_ref),
        (res_hbm, res_ref), (dir_hbm, dir_ref), (sol_hbm, sol_ref)))]
    for copy in loads:
        copy.start()
    load_hits, load_noise, load_st, load_tb, load_res, load_dir, load_sol = loads
    pl.semaphore_wait(barrier, len(greet))

    for k, dz in NEAR:
        remote(dir_hbm, w_ref.at[c, 16 * (1 - dz) + me], a_send, a_recv.at[3 * k + dz + 1], at(k, 0, dz)).start()
    for m in (2, 1, 3):
        remote(dir_hbm, w_ref.at[c, 16 + me], a_send, s2_recv.at[1], at(0, m, 0)).start()
    halo = []
    edge = 16384 - 512
    for k, (dev, off, slot) in enumerate(((partner, other * edge, c), (side, c * edge, other))):
        off = pl.multiple_of(off, 128)
        halo.append(remote(hits_hbm, hn_ref.at[slot], h_send.at[2 * k], h_recv.at[slot], dev))
        halo.append(remote(st_hbm.at[:, :, pl.ds(off, 512)], sh_ref.at[slot], h_send.at[2 * k + 1],
                           h_recv.at[2 + slot], dev))
    for copy in halo:
        copy.start()

    def relay(k, dz):
        shard = w_ref.at[c, 16 * (1 - dz) + 4 * b + lax.rem(a + 4 - k, 4)]
        remote(shard, shard, a_send, a_recv.at[3 * k + dz + 1], partner).wait_recv()
        for m in (2, 1, 3):
            remote(shard, shard, a_send, s2_recv.at[1 - dz], at(0, m, 0)).start()

    load_hits.wait()
    ids = halves(c)
    gather_side(hits_ref, oh_ref, ids)
    for k, dz in RELAY[:3]:
        relay(k, dz)
    for k, dz in RELAY[3:]:
        relay(k, dz)
    load_noise.wait()
    bin_side(hits_ref, noise_ref, oht_ref, wt_ref)
    load_st.wait()
    own.wait()
    for k in range(2):
        remote(hits_hbm, hn_ref.at[k], h_send.at[0], h_recv.at[k], partner).wait_recv()
        remote(sh_ref.at[k], sh_ref.at[k], h_send.at[0], h_recv.at[2 + k], partner).wait_recv()
    first = jnp.logical_and(ty == 0, c == 0)
    last = jnp.logical_and(ty == 3, c == 1)
    one_hot_rows(oh_ref, jnp.where(first, 768, hn_ref[0]), 124, 0, ids)
    one_hot_rows(oh_ref, jnp.where(last, 768, hn_ref[1]), 0, 33, ids)

    pairs = []

    def swap(t):
        pltpu.make_async_copy(w_ref.at[c, 16 * t:16 * t + 12], w_ref.at[c, 16 * t:16 * t + 12], s2_recv.at[t]).wait()
        copy = remote(w_ref.at[c, 16 * t:16 * t + 16], w_ref.at[c, 16 * t:16 * t + 16], ap_send.at[t], ap_recv.at[t], partner)
        copy.start()
        pairs.append(copy)

    def fill(t, core, base):
        if core is other:
            remote(w_ref.at[other, 16 * t:16 * t + 16], w_ref.at[other, 16 * t:16 * t + 16],
                   ap_send.at[t], ap_recv.at[t], partner).wait_recv()
        for p in range(0, 16, 2):
            for k in range(3):
                both = jnp.concatenate([w_ref[core, 16 * t + p, k], w_ref[core, 16 * t + p + 1, k]], 0)
                hi, lo = split(both)
                rows = slice(base + 8 * p, base + 8 * p + 16)
                tab_ref[rows, 128 * k:128 * k + 128] = hi
                tab_ref[rows, 384 + 128 * k:512 + 128 * k] = lo

    swap(1)
    fill(1, c, 0)
    fill(1, other, 128)
    scan_samples(0, 256, tab_ref, st_ref, sh_ref, oh_ref, x_ref)
    swap(0)
    swap(2)
    for dz in (2, 6):
        pl.semaphore_signal(hand_sem, inc=1, device_id=at(0, 0, dz), device_id_type=MESH)
    fill(0, c, 256)
    fill(2, c, 384)
    scan_samples(256, 512, tab_ref, st_ref, sh_ref, oh_ref, x_ref)
    fill(0, other, 512)
    fill(2, other, 640)
    scan_samples(512, 768, tab_ref, st_ref, sh_ref, oh_ref, x_ref)
    load_tb.wait()
    noise_filter(x_ref, tb_ref, wt_ref, st_ref, v_ref)

    out_pairs = []

    def bin_and_swap(k):
        bin_map(k, oht_ref, v_ref, b_ref)
        out_pairs.append(remote(b_ref.at[other, k], pr_ref.at[k], cp_send.at[k], cp_recv.at[k], partner))
        out_pairs[k].start()

    def send_map(k):
        out_pairs[k].wait_recv()
        s_ref[k] = b_ref[c, k] + pr_ref[k]
        for m in (2, 1, 3):
            remote(s_ref.at[k, lax.rem(b + m, 4)], q_ref.at[k, m - 1], q_send, q_recv.at[k], at(0, m, 0)).start()

    def pass_map(k):
        pltpu.make_async_copy(q_ref.at[k], q_ref.at[k], q_recv.at[k]).wait()
        t_ref[k] = s_ref[k, b] + q_ref[k, 0] + q_ref[k, 1] + q_ref[k, 2]
        for t in (0, 2, 1):
            for n in (2, 1, 3, 0):
                src = t_ref.at[k, t, lax.rem(a + n, 4)]
                dst = r_ref.at[12 * k + 4 * t + a]
                if (n, t) == (0, 1):
                    pltpu.make_async_copy(src, dst, c_recv.at[k]).start()
                else:
                    remote(src, dst, c_send, c_recv.at[k], at(n, 0, t - 1)).start()

    bin_and_swap(0)
    bin_and_swap(1)
    send_map(0)
    bin_and_swap(2)
    send_map(1)
    send_map(2)
    pass_map(0)
    pass_map(1)
    pass_map(2)
    load_res.wait()
    load_dir.wait()
    load_sol.wait()
    image = []
    parts = [jnp.zeros((8, 128), F32)] * 4
    for k in range(3):
        pltpu.make_async_copy(r_ref.at[12 * k:12 * k + 12], r_ref.at[12 * k:12 * k + 12], c_recv.at[k]).wait()
        m = r_ref[12 * k]
        for p in range(1, 12):
            m = m + r_ref[12 * k + p]
        image.append(m)
        res, dire = res_ref[k], dir_ref[k]
        parts = [p + v for p, v in zip(parts, (res * res, dire * m, res * m, m * m))]
    parts = [jnp.sum(p, axis=0, keepdims=True) for p in parts]
    part = lane_iota((1, 128)) // 32
    total = jnp.zeros((1, 128), F32)
    for k, p in enumerate(parts):
        p = p + pltpu.roll(p, 64, 1)
        p = p + pltpu.roll(p, 32, 1)
        total = jnp.where(part == k, p, total)
    n0_ref[...] = total
    cell = 8 * g + 2 * ty + c
    pltpu.make_async_copy(n0_ref, n1_ref.at[cell], n1_recv).start()
    for dx in (2, 1, 3, 0):
        for dy in (2, 1, 3, 0):
            for core in (other, c) if dx + dy else (other,):
                dev = (lax.rem(g + dx, 4), d, lax.rem(ty + dy, 4), core)
                remote(n0_ref, n1_ref.at[cell], n1_send, n1_recv, dev).start()
    pltpu.make_async_copy(n1_ref, n1_ref, n1_recv).wait()
    m1_ref[...] = jnp.sum(n1_ref[...], axis=0)
    pltpu.make_async_copy(m1_ref, n2_ref.at[d], n2_recv).start()
    pl.semaphore_wait(hand_sem, 2)
    for dz in (4, 3, 5, 2, 6, 1, 7):
        remote(m1_ref, n2_ref.at[d], n2_send, n2_recv, at(0, 0, dz)).start()
    for copy in halo + pairs + out_pairs:
        copy.wait_send()
    pltpu.make_async_copy(w_ref.at[0, 0:47], w_ref.at[0, 0:47], a_send).wait()
    pltpu.make_async_copy(q_ref, q_ref, q_send).wait()
    pltpu.make_async_copy(r_ref.at[0:33], r_ref.at[0:33], c_send).wait()
    pltpu.make_async_copy(n2_ref, n2_ref, n2_recv).wait()
    sums = jnp.sum(n2_ref[...], axis=0)
    old_norm, curvature, cross_term, image_norm = (
        jnp.sum(jnp.where(part == k, sums, 0.0), axis=1, keepdims=True) for k in range(4))
    step = old_norm / curvature
    new_norm = old_norm - 2.0 * step * cross_term + step * step * image_norm
    ratio = new_norm / old_norm
    for k in range(3):
        dire = dir_ref[k]
        out_ref[0, k] = sol_ref[k] + step * dire
        nr = res_ref[k] - step * image[k]
        out_ref[1, k] = nr
        out_ref[2, k] = nr + ratio * dire
    pltpu.make_async_copy(n1_ref.at[0:31], n1_ref.at[0:31], n1_send).wait()
    pltpu.make_async_copy(n2_ref.at[0:7], n2_ref.at[0:7], n2_send).wait()


def step_kernel(sol, res, dire, hits, st, noise, tb):
    hbm = pl.BlockSpec(memory_space=pltpu.HBM)
    dma = pltpu.SemaphoreType.DMA
    scratch = [
        pltpu.VMEM((2, 48, 3, 8, 128), F32), pltpu.VMEM((768, 768), BF), pltpu.VMEM((4, 544, 768), BF),
        pltpu.VMEM((768, 2048), BF), pltpu.VMEM((3, 16, 256), F32), pltpu.VMEM((544, 512), F32),
        pltpu.VMEM((2048, 768), BF), pltpu.VMEM((2, 3, 4, 3, 4, 8, 128), F32),
        pltpu.VMEM((3, 4, 3, 4, 8, 128), F32), pltpu.VMEM((3, 4, 3, 4, 8, 128), F32),
        pltpu.VMEM((3, 3, 3, 4, 8, 128), F32), pltpu.VMEM((3, 3, 4, 8, 128), F32), pltpu.VMEM((36, 8, 128), F32),
        pltpu.VMEM((2, 16, 16384), jnp.int32), pltpu.VMEM((8, 512, 256), BF),
        pltpu.VMEM((2, 2, 16, 512), jnp.int32), pltpu.VMEM((2, 16, 128), jnp.int32),
        pltpu.VMEM((1, 128), F32), pltpu.VMEM((32, 1, 128), F32), pltpu.VMEM((1, 128), F32),
        pltpu.VMEM((8, 1, 128), F32), pltpu.VMEM((3, 8, 128), F32), pltpu.VMEM((3, 8, 128), F32),
        pltpu.VMEM((3, 8, 128), F32), pltpu.VMEM((16, 128), jnp.int32), pltpu.VMEM((16, 512), F32),
        dma((7,)), dma, dma, dma((12,)), dma((3,)), dma((3,)), dma((3,)), dma((4,)), dma((4,)),
        dma, dma((3,)), dma, dma((3,)), dma((3,)), dma((3,)), dma, dma, dma, dma,
        pltpu.SemaphoreType.REGULAR,
    ]
    return pl.pallas_call(
        kernel, out_shape=jax.ShapeDtypeStruct((3, 3, 8, 128), F32),
        in_specs=[hbm] * 7, out_specs=pl.BlockSpec(memory_space=pltpu.VMEM), scratch_shapes=scratch,
        compiler_params=pltpu.CompilerParams(
            vmem_limit_bytes=40 << 20, collective_id=0, has_side_effects=True),
    )(*(pltpu.with_memory_space_constraint(a, pltpu.HBM) for a in (sol, res, dire, hits, st, noise, tb)))


def shards(map_solution, map_residual, map_direction, hits, stokes_int, inv_noise):
    out = step_kernel(map_solution[:, 0], map_residual[:, 0], map_direction[:, 0], hits, stokes_int, inv_noise,
                      jnp.asarray(tables()))
    return (out[0][:, None], out[1][:, None], out[2][:, None])


def solution(mesh):
    torus = Mesh(
        mesh.devices.reshape(mesh.shape["group"], mesh.shape["det"], 4, 2),
        ("group", "det", "tm_0", "tm_1"),
    )
    TM = ("tm_0", "tm_1")
    tile = P(None, "det", ("group",) + TM, None)
    in_specs = (tile, tile, tile, P(("group", "det"), TM), P(None, ("group", "det"), TM), P(("group", "det"), None))
    return jax.shard_map(shards, mesh=torus, in_specs=in_specs, out_specs=(tile, tile, tile), check_vma=False)
```

```python
import math
import numpy as np
import jax, jax.numpy as jnp
from jax import lax
from jax.experimental import pallas as pl
from jax.experimental.pallas import tpu as pltpu
from jax.sharding import Mesh
from jax.sharding import PartitionSpec as P

BF = jnp.bfloat16
F32 = jnp.float32

def basis_tables():
    n = np.arange(256)[None, :]
    k = np.arange(256)[:, None]
    kk = np.where(k <= 128, k, k - 128)
    ang = 2 * np.pi * ((kk * n) % 256) / 256
    fe = np.where(k <= 128, np.cos(ang), np.sin(ang))
    fe = fe * np.where((k == 0) | (k == 128), math.sqrt(1 / 256), math.sqrt(2 / 256))
    kk = k % 128
    ang = 2 * np.pi * (((2 * kk + 1) * n) % 512) / 512
    fo = np.where(k < 128, np.cos(ang), np.sin(ang)) * math.sqrt(2 / 256)
    ang = 2 * np.pi * (((2 * k + 1) * n) % 1024) / 1024
    fc = np.cos(ang) / 16
    fs = np.sin(ang) / 16
    fs[:, 0] = np.where(np.arange(256) % 2 == 0, 1, -1) / 16
    return [fe, fo, fc, fs]

def split_np(a):
    a = np.asarray(a, np.float32)
    hi = a.astype(BF)
    lo = (a - hi.astype(np.float32)).astype(BF)
    return hi, lo

def tables():
    fe, fo, fc, fs = basis_tables()
    out = []
    for m in (fe.T, fo.T, fc.T, fs.T, fe * 0.5, fo * 0.5, fc, fs):
        hi, lo = split_np(m)
        out.append(np.concatenate([hi, lo], 0))
    return np.stack(out)

def split(x):
    hi = x.astype(BF)
    lo = (x - hi.astype(F32)).astype(BF)
    return hi, lo

def dot(a, b):
    return jnp.dot(a, b, preferred_element_type=F32)

def dot3(x, tab):
    hi, lo = split(x)
    th = tab[0:256, :]
    tl = tab[256:512, :]
    return dot(hi, th) + dot(hi, tl) + dot(lo, th)

def lane_iota(shape):
    return lax.broadcasted_iota(jnp.int32, shape, len(shape) - 1)

def take(x, idx):
    return jnp.take_along_axis(x, idx, axis=1)

def reverse256(a, b):
    lane = lane_iota(a.shape)
    p = lax.rem(128 - lane, 128)
    ap, bp = take(a, p), take(b, p)
    z = lane == 0
    return jnp.where(z, ap, bp), jnp.where(z, bp, ap)

def weight_tables(w):
    lane = lane_iota((16, 128))
    blk = [w[:, 128 * b:128 * b + 128] for b in range(4)]
    def pick(stride, off, blocks):
        per = 128 // stride
        idx = stride * lax.rem(lane, per) + off
        out = take(blk[blocks[0]], idx)
        for t, b in enumerate(blocks[1:], 1):
            out = jnp.where(lane // per == t, take(blk[b], idx), out)
        return out
    w0 = pick(4, 0, (0, 1, 2, 3))
    w2 = pick(4, 2, (0, 1, 2, 3))
    last = jnp.broadcast_to(w[:, 511:512], (16, 128))
    we = (w0, jnp.where(lane == 0, last, w0))
    wo = (w2, w2)
    wd = (pick(2, 1, (0, 1)), pick(2, 1, (2, 3)))
    return we, wo, wd

def hit_rows(hits):
    h = hits.astype(F32)
    a = jnp.floor(h * (1.0 / 256.0))
    b = h - 256.0 * a
    both = jnp.concatenate([a, b], 0).astype(BF)
    row = lax.broadcasted_iota(jnp.int32, (128, 2048), 0)
    col = lax.broadcasted_iota(jnp.int32, (128, 2048), 1)
    want = 4 * ((col // 16) % 32) + col // 512
    p = jnp.where(row == want, 1.0, 0.0).astype(BF)
    y = dot(both, p)
    y = 256.0 * y[:16] + y[16:]
    i = lax.broadcasted_iota(jnp.int32, (16, 2048), 0)
    c = lax.broadcasted_iota(jnp.int32, (16, 2048), 1)
    return jnp.sum(jnp.where(i == c % 16, y, 0.0), axis=0, keepdims=True)

def block_ids(tile, core):
    lane = lane_iota((16, 128))
    place, row = lane // 8, lax.rem(lane, 8)
    chip = (1 - core) * (4 * lax.rem(place, 4) + place // 4) + core * place
    return 256 * tile + 16 * chip + 8 * core + row


def halves(core):
    return [block_ids(t, k) for t, k in ((1, core), (1, 1 - core), (0, core), (2, core), (0, 1 - core), (2, 1 - core))]


def one_hot_rows(oh_ref, hits, cols, s, ids):
    for j in range(4):
        hb = jnp.broadcast_to(hits[:, cols + j:cols + j + 1], (16, 128))
        for k in range(6):
            oh_ref[j, 16 * s:16 * s + 16, 128 * k:128 * k + 128] = jnp.where(hb == ids[k], 1.0, 0.0).astype(BF)


def gather_side(hits_ref, oh_ref, ids):
    hits = hits_ref[...]
    for s in range(32):
        one_hot_rows(oh_ref, hits, 4 * s, s + 1, ids)


def row_side(hits_ref, hrow_ref):
    hits = hits_ref[...]
    hrow_ref[...] = hit_rows(hits)


def bin_side(core, hrow_ref, oht_ref):
    sub = lax.broadcasted_iota(jnp.int32, (16, 128), 0)
    pattern = (lax.rem(sub, 8) + (sub // 8) * (16 if core else 64) + 8 * core).astype(F32)

    def rows(t, carry):
        second, tile, first = t // 6, lax.rem(t, 6) // 2, 2 * lax.rem(t, 2)
        chip = 4 * second + first if core else 4 * first + second
        want = pattern + (256 * tile + 16 * chip).astype(F32)
        for k in range(16):
            hb = hrow_ref[:, 128 * k:128 * k + 128]
            oht_ref[core, pl.ds(pl.multiple_of(t * 16, 16), 16), 128 * k:128 * k + 128] = jnp.where(
                want == hb, 1.0, 0.0).astype(BF)
        return carry
    lax.fori_loop(0, 24, rows, 0)


def weight_side(noise_ref, wt_ref):
    we, wo, wd = weight_tables(noise_ref[...])
    for t, (a, b) in enumerate((we, wo, wd)):
        wt_ref[t, :, 0:128] = a
        wt_ref[t, :, 128:256] = b

def scan_samples(lo, hi, tab_ref, st_ref, sh_ref, oh_ref, x_ref):
    def one(j, carry):
        off = j * 128
        g = dot(oh_ref[j, :, lo:hi], tab_ref[lo:hi, :])
        gi = g[:, 0:128] + g[:, 384:512]
        gq = g[:, 128:256] + g[:, 512:640]
        gu = g[:, 256:384] + g[:, 640:768]
        for s in range(34):
            r = slice(16 * s, 16 * s + 16)
            if s == 0 or s == 33:
                e = 0 if s == 0 else 1
                q = sh_ref[e, 0, :, pl.ds(off, 128)]
                u = sh_ref[e, 1, :, pl.ds(off, 128)]
            else:
                o = off + 512 * (s - 1)
                q = st_ref[0, :, pl.ds(o, 128)]
                u = st_ref[1, :, pl.ds(o, 128)]
            q, u = q.astype(F32), u.astype(F32)
            v = gi[r] + q * gq[r] + u * gu[r]
            x_ref[r, pl.ds(off, 128)] = v if lo == 0 else x_ref[r, pl.ds(off, 128)] + v
        return carry
    for j in range(4):
        one(j, 0)

def noise_filter(x_ref, tb_ref, wt_ref, st_ref, v_ref):
    M = 128
    def chunk(t, carry):
        base = t * M
        def xs(c, d):
            return x_ref[pl.ds(base + 16 * d, M), 128 * c:128 * c + 128]
        u, v = [], []
        for c in range(4):
            y = 0.5 * (xs(c, 0) + xs(c, 2))
            x = xs(c, 1)
            u.append(x + y)
            v.append(x - y)
        ue = jnp.concatenate([u[0] + u[2], u[1] + u[3]], 1)
        uo = jnp.concatenate([u[0] - u[2], u[1] - u[3]], 1)
        r0, r1 = reverse256(v[2], v[3])
        z = lane_iota((M, 128)) == 0
        vc = jnp.concatenate([v[0] - jnp.where(z, 0.0, r0), v[1] - r1], 1)
        vs = jnp.concatenate([jnp.where(z, r0, v[0] + r0), v[1] + r1], 1)
        outs = []
        for t_, (a, wi) in enumerate(((ue, 0), (uo, 1), (vc, 2), (vs, 2))):
            c = dot3(a, tb_ref[t_])
            c = (c.reshape(M // 16, 16, 256) * wt_ref[wi][None]).reshape(M, 256)
            outs.append(dot3(c, tb_ref[4 + t_]))
        ae, ao, oc, os_ = outs
        oc0, oc1, os0, os1 = oc[:, :128], oc[:, 128:], os_[:, :128], os_[:, 128:]
        p0, p1 = jnp.where(z, os0, os0 - oc0), os1 - oc1
        d2, d3 = reverse256(p0, p1)
        d0, d1 = oc0 + jnp.where(z, 0.0, os0), oc1 + os1
        ae0, ae1, ao0, ao1 = ae[:, :128], ae[:, 128:], ao[:, :128], ao[:, 128:]
        for j, f in enumerate((ae0 + ao0 + d0, ae1 + ao1 + d1, ae0 - ao0 + d2, ae1 - ao1 + d3)):
            for i in range(M // 16):
                s = t * (M // 16) + i
                o = 128 * j + 512 * s
                q = st_ref[0, :, o:o + 128].astype(F32)
                w = st_ref[1, :, o:o + 128].astype(F32)
                r = 512 * j + 16 * s
                fi = f[16 * i:16 * i + 16]
                scaled = fi * (1.0 / 2048.0)
                for k, val in enumerate((fi, q * scaled, w * scaled)):
                    hi, lo = split(val)
                    v_ref[r:r + 16, 256 * k:256 * k + 128] = hi
                    v_ref[r:r + 16, 256 * k + 128:256 * k + 256] = lo
        return carry
    for t in range(512 // M):
        chunk(t, 0)


def bin_half(core, k, oht_ref, v_ref):
    g = dot(oht_ref[core], v_ref[:, 256 * k:256 * k + 256])
    return g[:, 0:128] + g[:, 128:256]


MESH = pl.DeviceIdType.MESH
NEAR = [(k, dz) for k in (2, 1, 3, 0) for dz in (1, -1, 0) if (k, dz) != (0, 0)]
RELAY = [(1, 0), (3, 0), (2, 0), (0, 1), (0, -1), (1, 1), (1, -1), (3, 1), (3, -1), (2, 1), (2, -1)]


def remote(src, dst, send, recv, where):
    return pltpu.make_async_remote_copy(
        src_ref=src, dst_ref=dst, send_sem=send, recv_sem=recv, device_id=where, device_id_type=MESH)


def kernel(sol_hbm, res_hbm, dir_hbm, hits_hbm, st_hbm, noise_hbm, tb_hbm, out_ref,
           w_ref, tab_ref, oh_ref, oht_ref, wt_ref, x_ref, v_ref, b_ref, pr_ref, s_ref, q_ref, t_ref, r_ref,
           st_ref, tb_ref, sh_ref, hn_ref, n0_ref, n1_ref, m1_ref, n2_ref, sol_ref, res_ref, dir_ref, hits_ref,
           noise_ref, hrow_ref, in_sem, own_sem, a_send, a_recv, s2_recv, ap_send, ap_recv, h_send, h_recv,
           q_send, q_recv, c_send, c_recv, cp_send, cp_recv, n1_send, n1_recv, n2_send, n2_recv, hand_sem):
    g, d, ty, c = (lax.axis_index(a) for a in ("group", "det", "tm_0", "tm_1"))
    other = 1 - c
    a = g * other + ty * c
    b = ty * other + g * c
    me = 4 * b + a
    partner = (g, d, ty, other)
    side = (g, d, lax.rem(ty + 3 + 2 * c, 4), other)

    def at(k, m, dz):
        pa, pb = lax.rem(a + k, 4), lax.rem(b + m, 4)
        return (pa * other + pb * c, lax.rem(d + dz + 8, 8), pb * other + pa * c, c)

    greet = [at(k, 0, dz) for k, dz in NEAR] + [at(0, m, 0) for m in (2, 1, 3)] + [side, partner]
    barrier = pltpu.get_barrier_semaphore()
    for dev in greet:
        pl.semaphore_signal(barrier, inc=1, device_id=dev, device_id_type=MESH)
    own = pltpu.make_async_copy(dir_hbm, w_ref.at[c, 16 + me], own_sem)
    own.start()
    loads = [pltpu.make_async_copy(src, dst, in_sem.at[k]) for k, (src, dst) in enumerate((
        (hits_hbm, hits_ref), (noise_hbm, noise_ref), (st_hbm, st_ref), (tb_hbm, tb_ref),
        (res_hbm, res_ref), (dir_hbm, dir_ref), (sol_hbm, sol_ref)))]
    for copy in loads:
        copy.start()
    load_hits, load_noise, load_st, load_tb, load_res, load_dir, load_sol = loads
    pl.semaphore_wait(barrier, len(greet))

    for k, dz in NEAR:
        remote(dir_hbm, w_ref.at[c, 16 * (1 - dz) + me], a_send, a_recv.at[3 * k + dz + 1], at(k, 0, dz)).start()
    for m in (2, 1, 3):
        remote(dir_hbm, w_ref.at[c, 16 + me], a_send, s2_recv.at[1], at(0, m, 0)).start()
    halo = []
    edge = 16384 - 512
    for k, (dev, off, slot) in enumerate(((partner, other * edge, c), (side, c * edge, other))):
        off = pl.multiple_of(off, 128)
        halo.append(remote(hits_hbm, hn_ref.at[slot], h_send.at[2 * k], h_recv.at[slot], dev))
        halo.append(remote(st_hbm.at[:, :, pl.ds(off, 512)], sh_ref.at[slot], h_send.at[2 * k + 1],
                           h_recv.at[2 + slot], dev))
    for copy in halo:
        copy.start()

    def relay(k, dz):
        shard = w_ref.at[c, 16 * (1 - dz) + 4 * b + lax.rem(a + 4 - k, 4)]
        remote(shard, shard, a_send, a_recv.at[3 * k + dz + 1], partner).wait_recv()
        for m in (2, 1, 3):
            remote(shard, shard, a_send, s2_recv.at[1 - dz], at(0, m, 0)).start()

    load_hits.wait()
    ids = halves(c)
    gather_side(hits_ref, oh_ref, ids)
    row_side(hits_ref, hrow_ref)
    bin_side(0, hrow_ref, oht_ref)
    for k, dz in RELAY[:3]:
        relay(k, dz)
    for k, dz in RELAY[3:]:
        relay(k, dz)
    bin_side(1, hrow_ref, oht_ref)
    load_noise.wait()
    weight_side(noise_ref, wt_ref)
    load_st.wait()
    own.wait()
    for k in range(2):
        remote(hits_hbm, hn_ref.at[k], h_send.at[0], h_recv.at[k], partner).wait_recv()
        remote(sh_ref.at[k], sh_ref.at[k], h_send.at[0], h_recv.at[2 + k], partner).wait_recv()
    first = jnp.logical_and(ty == 0, c == 0)
    last = jnp.logical_and(ty == 3, c == 1)
    one_hot_rows(oh_ref, jnp.where(first, 768, hn_ref[0]), 124, 0, ids)
    one_hot_rows(oh_ref, jnp.where(last, 768, hn_ref[1]), 0, 33, ids)

    pairs = []

    def swap(t):
        pltpu.make_async_copy(w_ref.at[c, 16 * t:16 * t + 12], w_ref.at[c, 16 * t:16 * t + 12], s2_recv.at[t]).wait()
        copy = remote(w_ref.at[c, 16 * t:16 * t + 16], w_ref.at[c, 16 * t:16 * t + 16], ap_send.at[t], ap_recv.at[t], partner)
        copy.start()
        pairs.append(copy)

    def fill(t, core, base):
        if core is other:
            remote(w_ref.at[other, 16 * t:16 * t + 16], w_ref.at[other, 16 * t:16 * t + 16],
                   ap_send.at[t], ap_recv.at[t], partner).wait_recv()
        for p in range(0, 16, 2):
            for k in range(3):
                both = jnp.concatenate([w_ref[core, 16 * t + p, k], w_ref[core, 16 * t + p + 1, k]], 0)
                hi, lo = split(both if k == 0 else both * (1.0 / 2048.0))
                rows = slice(base + 8 * p, base + 8 * p + 16)
                tab_ref[rows, 128 * k:128 * k + 128] = hi
                tab_ref[rows, 384 + 128 * k:512 + 128 * k] = lo

    swap(1)
    fill(1, c, 0)
    fill(1, other, 128)
    scan_samples(0, 256, tab_ref, st_ref, sh_ref, oh_ref, x_ref)
    swap(0)
    swap(2)
    for dz in (2, 6):
        pl.semaphore_signal(hand_sem, inc=1, device_id=at(0, 0, dz), device_id_type=MESH)
    fill(0, c, 256)
    fill(2, c, 384)
    scan_samples(256, 512, tab_ref, st_ref, sh_ref, oh_ref, x_ref)
    fill(0, other, 512)
    fill(2, other, 640)
    scan_samples(512, 768, tab_ref, st_ref, sh_ref, oh_ref, x_ref)
    load_tb.wait()
    noise_filter(x_ref, tb_ref, wt_ref, st_ref, v_ref)

    out_pairs = []

    def give(k):
        out_pairs.append(remote(b_ref.at[0, k], pr_ref.at[k], cp_send.at[k], cp_recv.at[k], partner))
        out_pairs[k].start()

    def send_map(k):
        out_pairs[k].wait_recv()
        for p in range(4):
            rows = slice(96 * p, 96 * p + 96)
            s_ref[k, p] = b_ref[1, k, rows] + pr_ref[k, rows]
        for m in (2, 1, 3):
            remote(s_ref.at[k, lax.rem(b + m, 4)], q_ref.at[k, m - 1], q_send, q_recv.at[k], at(0, m, 0)).start()

    def pass_map(k):
        pltpu.make_async_copy(q_ref.at[k], q_ref.at[k], q_recv.at[k]).wait()
        for p in range(12):
            rows = slice(8 * p, 8 * p + 8)
            t_ref[p // 4, p % 4, k] = s_ref[k, b, rows] + q_ref[k, 0, rows] + q_ref[k, 1, rows] + q_ref[k, 2, rows]

    def pass_on():
        for t in (0, 2, 1):
            for n in (2, 1, 3, 0):
                src = t_ref.at[t, lax.rem(a + n, 4)]
                dst = r_ref.at[4 * t + a]
                if (n, t) == (0, 1):
                    pltpu.make_async_copy(src, dst, c_recv).start()
                else:
                    remote(src, dst, c_send, c_recv, at(n, 0, t - 1)).start()

    first_two = [bin_half(other, k, oht_ref, v_ref) for k in (0, 1)]
    for k in (0, 1):
        b_ref[0, k] = first_two[k]
    give(0)
    give(1)
    last, mine = bin_half(other, 2, oht_ref, v_ref), bin_half(c, 0, oht_ref, v_ref)
    b_ref[0, 2] = last
    b_ref[1, 0] = mine
    give(2)
    send_map(0)
    mine = [bin_half(c, k, oht_ref, v_ref) for k in (1, 2)]
    for k in (1, 2):
        b_ref[1, k] = mine[k - 1]
    send_map(1)
    send_map(2)
    pass_map(0)
    pass_map(1)
    pass_map(2)
    pass_on()
    load_res.wait()
    load_dir.wait()
    load_sol.wait()
    image = []
    parts = [jnp.zeros((8, 128), F32)] * 4
    pltpu.make_async_copy(r_ref, r_ref, c_recv).wait()
    for k in range(3):
        m = r_ref[0, k]
        for p in range(1, 12):
            m = m + r_ref[p, k]
        image.append(m)
        res, dire = res_ref[k], dir_ref[k]
        parts = [p + v for p, v in zip(parts, (res * res, dire * m, res * m, m * m))]
    parts = [jnp.sum(p, axis=0, keepdims=True) for p in parts]
    part = lane_iota((1, 128)) // 32
    total = jnp.zeros((1, 128), F32)
    for k, p in enumerate(parts):
        p = p + pltpu.roll(p, 64, 1)
        p = p + pltpu.roll(p, 32, 1)
        total = jnp.where(part == k, p, total)
    n0_ref[...] = total
    cell = 8 * g + 2 * ty + c
    pltpu.make_async_copy(n0_ref, n1_ref.at[cell], n1_recv).start()
    for dx in (2, 1, 3, 0):
        for dy in (2, 1, 3, 0):
            for core in (other, c) if dx + dy else (other,):
                dev = (lax.rem(g + dx, 4), d, lax.rem(ty + dy, 4), core)
                remote(n0_ref, n1_ref.at[cell], n1_send, n1_recv, dev).start()
    pltpu.make_async_copy(n1_ref, n1_ref, n1_recv).wait()
    m1_ref[...] = jnp.sum(n1_ref[...], axis=0)
    pltpu.make_async_copy(m1_ref, n2_ref.at[d], n2_recv).start()
    pl.semaphore_wait(hand_sem, 2)
    for dz in (4, 3, 5, 2, 6, 1, 7):
        remote(m1_ref, n2_ref.at[d], n2_send, n2_recv, at(0, 0, dz)).start()
    for copy in halo + pairs + out_pairs:
        copy.wait_send()
    pltpu.make_async_copy(w_ref.at[0, 0:47], w_ref.at[0, 0:47], a_send).wait()
    pltpu.make_async_copy(q_ref, q_ref, q_send).wait()
    pltpu.make_async_copy(r_ref.at[0:11], r_ref.at[0:11], c_send).wait()
    pltpu.make_async_copy(n2_ref, n2_ref, n2_recv).wait()
    sums = jnp.sum(n2_ref[...], axis=0)
    old_norm, curvature, cross_term, image_norm = (
        jnp.sum(jnp.where(part == k, sums, 0.0), axis=1, keepdims=True) for k in range(4))
    step = old_norm / curvature
    new_norm = old_norm - 2.0 * step * cross_term + step * step * image_norm
    ratio = new_norm / old_norm
    for k in range(3):
        dire = dir_ref[k]
        out_ref[0, k] = sol_ref[k] + step * dire
        nr = res_ref[k] - step * image[k]
        out_ref[1, k] = nr
        out_ref[2, k] = nr + ratio * dire
    pltpu.make_async_copy(n1_ref.at[0:31], n1_ref.at[0:31], n1_send).wait()
    pltpu.make_async_copy(n2_ref.at[0:7], n2_ref.at[0:7], n2_send).wait()


def step_kernel(sol, res, dire, hits, st, noise, tb):
    hbm = pl.BlockSpec(memory_space=pltpu.HBM)
    dma = pltpu.SemaphoreType.DMA
    scratch = [
        pltpu.VMEM((2, 48, 3, 8, 128), F32), pltpu.VMEM((768, 768), BF), pltpu.VMEM((4, 544, 768), BF),
        pltpu.VMEM((2, 384, 2048), BF), pltpu.VMEM((3, 16, 256), F32), pltpu.VMEM((544, 512), F32),
        pltpu.VMEM((2048, 768), BF), pltpu.VMEM((2, 3, 384, 128), F32),
        pltpu.VMEM((3, 384, 128), F32), pltpu.VMEM((3, 4, 96, 128), F32),
        pltpu.VMEM((3, 3, 96, 128), F32), pltpu.VMEM((3, 4, 3, 8, 128), F32), pltpu.VMEM((12, 3, 8, 128), F32),
        pltpu.VMEM((2, 16, 16384), jnp.int32), pltpu.VMEM((8, 512, 256), BF),
        pltpu.VMEM((2, 2, 16, 512), jnp.int32), pltpu.VMEM((2, 16, 128), jnp.int32),
        pltpu.VMEM((1, 128), F32), pltpu.VMEM((32, 1, 128), F32), pltpu.VMEM((1, 128), F32),
        pltpu.VMEM((8, 1, 128), F32), pltpu.VMEM((3, 8, 128), F32), pltpu.VMEM((3, 8, 128), F32),
        pltpu.VMEM((3, 8, 128), F32), pltpu.VMEM((16, 128), jnp.int32), pltpu.VMEM((16, 512), F32),
        pltpu.VMEM((1, 2048), F32),
        dma((7,)), dma, dma, dma((12,)), dma((3,)), dma((3,)), dma((3,)), dma((4,)), dma((4,)),
        dma, dma((3,)), dma, dma, dma((3,)), dma((3,)), dma, dma, dma, dma,
        pltpu.SemaphoreType.REGULAR,
    ]
    return pl.pallas_call(
        kernel, out_shape=jax.ShapeDtypeStruct((3, 3, 8, 128), F32),
        in_specs=[hbm] * 7, out_specs=pl.BlockSpec(memory_space=pltpu.VMEM), scratch_shapes=scratch,
        compiler_params=pltpu.CompilerParams(
            vmem_limit_bytes=40 << 20, collective_id=0, has_side_effects=True),
    )(*(pltpu.with_memory_space_constraint(a, pltpu.HBM) for a in (sol, res, dire, hits, st, noise, tb)))


def shards(map_solution, map_residual, map_direction, hits, stokes_int, inv_noise):
    out = step_kernel(map_solution[:, 0], map_residual[:, 0], map_direction[:, 0], hits, stokes_int, inv_noise,
                      jnp.asarray(tables()))
    return (out[0][:, None], out[1][:, None], out[2][:, None])


def solution(mesh):
    torus = Mesh(
        mesh.devices.reshape(mesh.shape["group"], mesh.shape["det"], 4, 2),
        ("group", "det", "tm_0", "tm_1"),
    )
    TM = ("tm_0", "tm_1")
    tile = P(None, "det", ("group",) + TM, None)
    in_specs = (tile, tile, tile, P(("group", "det"), TM), P(None, ("group", "det"), TM), P(("group", "det"), None))
    return jax.shard_map(shards, mesh=torus, in_specs=in_specs, out_specs=(tile, tile, tile), check_vma=False)
```

```python
import math
import numpy as np
import jax, jax.numpy as jnp
from jax import lax
from jax.experimental import pallas as pl
from jax.experimental.pallas import tpu as pltpu
from jax.sharding import Mesh
from jax.sharding import PartitionSpec as P

BF = jnp.bfloat16
F32 = jnp.float32

def basis_tables():
    n = np.arange(256)[None, :]
    k = np.arange(256)[:, None]
    kk = np.where(k <= 128, k, k - 128)
    ang = 2 * np.pi * ((kk * n) % 256) / 256
    fe = np.where(k <= 128, np.cos(ang), np.sin(ang))
    fe = fe * np.where((k == 0) | (k == 128), math.sqrt(1 / 256), math.sqrt(2 / 256))
    kk = k % 128
    ang = 2 * np.pi * (((2 * kk + 1) * n) % 512) / 512
    fo = np.where(k < 128, np.cos(ang), np.sin(ang)) * math.sqrt(2 / 256)
    ang = 2 * np.pi * (((2 * k + 1) * n) % 1024) / 1024
    fc = np.cos(ang) / 16
    fs = np.sin(ang) / 16
    fs[:, 0] = np.where(np.arange(256) % 2 == 0, 1, -1) / 16
    return [fe, fo, fc, fs]

def split_np(a):
    a = np.asarray(a, np.float32)
    hi = a.astype(BF)
    lo = (a - hi.astype(np.float32)).astype(BF)
    return hi, lo

def tables():
    fe, fo, fc, fs = basis_tables()
    out = []
    for m in (fe.T, fo.T, fc.T, fs.T, fe * 0.5, fo * 0.5, fc, fs):
        hi, lo = split_np(m)
        out.append(np.concatenate([hi, lo], 0))
    return np.stack(out)

def split(x):
    hi = x.astype(BF)
    lo = (x - hi.astype(F32)).astype(BF)
    return hi, lo

def dot(a, b):
    return jnp.dot(a, b, preferred_element_type=F32)

def dot3(x, tab):
    hi, lo = split(x)
    th = tab[0:256, :]
    tl = tab[256:512, :]
    return dot(hi, th) + dot(hi, tl) + dot(lo, th)

def lane_iota(shape):
    return lax.broadcasted_iota(jnp.int32, shape, len(shape) - 1)

def take(x, idx):
    return jnp.take_along_axis(x, idx, axis=1)

def reverse256(a, b):
    lane = lane_iota(a.shape)
    p = lax.rem(128 - lane, 128)
    ap, bp = take(a, p), take(b, p)
    z = lane == 0
    return jnp.where(z, ap, bp), jnp.where(z, bp, ap)

def weight_tables(w):
    lane = lane_iota((16, 128))
    blk = [w[:, 128 * b:128 * b + 128] for b in range(4)]
    def pick(stride, off, blocks):
        per = 128 // stride
        idx = stride * lax.rem(lane, per) + off
        out = take(blk[blocks[0]], idx)
        for t, b in enumerate(blocks[1:], 1):
            out = jnp.where(lane // per == t, take(blk[b], idx), out)
        return out
    w0 = pick(4, 0, (0, 1, 2, 3))
    w2 = pick(4, 2, (0, 1, 2, 3))
    last = jnp.broadcast_to(w[:, 511:512], (16, 128))
    we = (w0, jnp.where(lane == 0, last, w0))
    wo = (w2, w2)
    wd = (pick(2, 1, (0, 1)), pick(2, 1, (2, 3)))
    return we, wo, wd

def hit_rows(hits):
    h = hits.astype(F32)
    a = jnp.floor(h * (1.0 / 256.0))
    b = h - 256.0 * a
    both = jnp.concatenate([a, b], 0).astype(BF)
    row = lax.broadcasted_iota(jnp.int32, (128, 2048), 0)
    col = lax.broadcasted_iota(jnp.int32, (128, 2048), 1)
    want = 4 * ((col // 16) % 32) + col // 512
    p = jnp.where(row == want, 1.0, 0.0).astype(BF)
    y = dot(both, p)
    y = 256.0 * y[:16] + y[16:]
    i = lax.broadcasted_iota(jnp.int32, (16, 2048), 0)
    c = lax.broadcasted_iota(jnp.int32, (16, 2048), 1)
    return jnp.sum(jnp.where(i == c % 16, y, 0.0), axis=0, keepdims=True)

def block_ids(tile, core):
    lane = lane_iota((16, 128))
    place, row = lane // 8, lax.rem(lane, 8)
    chip = (1 - core) * (4 * lax.rem(place, 4) + place // 4) + core * place
    return 256 * tile + 16 * chip + 8 * core + row


def halves(core):
    return [block_ids(t, k) for t, k in ((1, core), (1, 1 - core), (0, core), (2, core), (0, 1 - core), (2, 1 - core))]


def one_hot_rows(oh_ref, hits, cols, s, ids):
    for j in range(4):
        hb = jnp.broadcast_to(hits[:, cols + j:cols + j + 1], (16, 128))
        for k in range(6):
            oh_ref[j, 16 * s:16 * s + 16, 128 * k:128 * k + 128] = jnp.where(hb == ids[k], 1.0, 0.0).astype(BF)


def gather_side(hits_ref, oh_ref, ids):
    hits = hits_ref[...]
    for s in range(32):
        one_hot_rows(oh_ref, hits, 4 * s, s + 1, ids)


def row_side(hits_ref, hrow_ref):
    hits = hits_ref[...]
    hrow_ref[...] = hit_rows(hits)


def bin_side(core, hrow_ref, oht_ref):
    sub = lax.broadcasted_iota(jnp.int32, (16, 128), 0)
    pattern = (lax.rem(sub, 8) + (sub // 8) * (16 if core else 64) + 8 * core).astype(F32)

    def rows(t, carry):
        second, tile, first = t // 6, lax.rem(t, 6) // 2, 2 * lax.rem(t, 2)
        chip = 4 * second + first if core else 4 * first + second
        want = pattern + (256 * tile + 16 * chip).astype(F32)
        for k in range(16):
            hb = hrow_ref[:, 128 * k:128 * k + 128]
            oht_ref[core, pl.ds(pl.multiple_of(t * 16, 16), 16), 128 * k:128 * k + 128] = jnp.where(
                want == hb, 1.0, 0.0).astype(BF)
        return carry
    lax.fori_loop(0, 24, rows, 0)


def weight_side(noise_ref, wt_ref):
    we, wo, wd = weight_tables(noise_ref[...])
    for t, (a, b) in enumerate((we, wo, wd)):
        wt_ref[t, :, 0:128] = a
        wt_ref[t, :, 128:256] = b

def scan_samples(lo, hi, tab_ref, st_ref, sh_ref, oh_ref, x_ref):
    def one(j, carry):
        off = j * 128
        g = dot(oh_ref[j, :, lo:hi], tab_ref[lo:hi, :])
        gi = g[:, 0:128] + g[:, 384:512]
        gq = g[:, 128:256] + g[:, 512:640]
        gu = g[:, 256:384] + g[:, 640:768]
        for s in range(34):
            r = slice(16 * s, 16 * s + 16)
            if s == 0 or s == 33:
                e = 0 if s == 0 else 1
                q = sh_ref[e, 0, :, pl.ds(off, 128)]
                u = sh_ref[e, 1, :, pl.ds(off, 128)]
            else:
                o = off + 512 * (s - 1)
                q = st_ref[0, :, pl.ds(o, 128)]
                u = st_ref[1, :, pl.ds(o, 128)]
            q, u = q.astype(F32), u.astype(F32)
            v = gi[r] + q * gq[r] + u * gu[r]
            x_ref[r, pl.ds(off, 128)] = v if lo == 0 else x_ref[r, pl.ds(off, 128)] + v
        return carry
    for j in range(4):
        one(j, 0)

def noise_filter(x_ref, tb_ref, wt_ref, st_ref, v_ref):
    M = 128
    def chunk(t, carry):
        base = t * M
        def xs(c, d):
            return x_ref[pl.ds(base + 16 * d, M), 128 * c:128 * c + 128]
        u, v = [], []
        for c in range(4):
            y = 0.5 * (xs(c, 0) + xs(c, 2))
            x = xs(c, 1)
            u.append(x + y)
            v.append(x - y)
        ue = jnp.concatenate([u[0] + u[2], u[1] + u[3]], 1)
        uo = jnp.concatenate([u[0] - u[2], u[1] - u[3]], 1)
        r0, r1 = reverse256(v[2], v[3])
        z = lane_iota((M, 128)) == 0
        vc = jnp.concatenate([v[0] - jnp.where(z, 0.0, r0), v[1] - r1], 1)
        vs = jnp.concatenate([jnp.where(z, r0, v[0] + r0), v[1] + r1], 1)
        outs = []
        for t_, (a, wi) in enumerate(((ue, 0), (uo, 1), (vc, 2), (vs, 2))):
            c = dot3(a, tb_ref[t_])
            c = (c.reshape(M // 16, 16, 256) * wt_ref[wi][None]).reshape(M, 256)
            outs.append(dot3(c, tb_ref[4 + t_]))
        ae, ao, oc, os_ = outs
        oc0, oc1, os0, os1 = oc[:, :128], oc[:, 128:], os_[:, :128], os_[:, 128:]
        p0, p1 = jnp.where(z, os0, os0 - oc0), os1 - oc1
        d2, d3 = reverse256(p0, p1)
        d0, d1 = oc0 + jnp.where(z, 0.0, os0), oc1 + os1
        ae0, ae1, ao0, ao1 = ae[:, :128], ae[:, 128:], ao[:, :128], ao[:, 128:]
        for j, f in enumerate((ae0 + ao0 + d0, ae1 + ao1 + d1, ae0 - ao0 + d2, ae1 - ao1 + d3)):
            for i in range(M // 16):
                s = t * (M // 16) + i
                o = 128 * j + 512 * s
                q = st_ref[0, :, o:o + 128].astype(F32)
                w = st_ref[1, :, o:o + 128].astype(F32)
                r = 512 * j + 16 * s
                fi = f[16 * i:16 * i + 16]
                scaled = fi * (1.0 / 2048.0)
                for k, val in enumerate((fi, q * scaled, w * scaled)):
                    hi, lo = split(val)
                    v_ref[r:r + 16, 256 * k:256 * k + 128] = hi
                    v_ref[r:r + 16, 256 * k + 128:256 * k + 256] = lo
        return carry
    for t in range(512 // M):
        chunk(t, 0)


def bin_half(core, k, oht_ref, v_ref):
    g = dot(oht_ref[core], v_ref[:, 256 * k:256 * k + 256])
    return g[:, 0:128] + g[:, 128:256]


MESH = pl.DeviceIdType.MESH
NEAR = [(k, dz) for k in (2, 1, 3, 0) for dz in (1, -1, 0) if (k, dz) != (0, 0)]
RELAY = [(1, 0), (3, 0), (2, 0), (0, 1), (0, -1), (1, 1), (1, -1), (3, 1), (3, -1), (2, 1), (2, -1)]


def remote(src, dst, send, recv, where):
    return pltpu.make_async_remote_copy(
        src_ref=src, dst_ref=dst, send_sem=send, recv_sem=recv, device_id=where, device_id_type=MESH)


def kernel(sol_hbm, res_hbm, dir_hbm, hits_hbm, st_hbm, noise_hbm, tb_hbm, out_ref,
           w_ref, tab_ref, oh_ref, oht_ref, wt_ref, x_ref, v_ref, b_ref, pr_ref, s_ref, q_ref, t_ref, r_ref,
           st_ref, tb_ref, sh_ref, hn_ref, n0_ref, n1_ref, m1_ref, n2_ref, map_ref, hits_ref,
           noise_ref, hrow_ref, in_sem, own_sem, a_send, a_recv, s2_recv, ap_send, ap_recv, h_send, h_recv,
           q_send, q_recv, c_send, c_recv, cp_send, cp_recv, n1_send, n1_recv, n2_send, n2_recv, hand_sem):
    g, d, ty, c = (lax.axis_index(a) for a in ("group", "det", "tm_0", "tm_1"))
    other = 1 - c
    a = g * other + ty * c
    b = ty * other + g * c
    me = 4 * b + a
    partner = (g, d, ty, other)
    side = (g, d, lax.rem(ty + 3 + 2 * c, 4), other)

    def at(k, m, dz):
        pa, pb = lax.rem(a + k, 4), lax.rem(b + m, 4)
        return (pa * other + pb * c, lax.rem(d + dz + 8, 8), pb * other + pa * c, c)

    greet = [at(k, 0, dz) for k, dz in NEAR] + [at(0, m, 0) for m in (2, 1, 3)] + [side, partner]
    barrier = pltpu.get_barrier_semaphore()
    for dev in greet:
        pl.semaphore_signal(barrier, inc=1, device_id=dev, device_id_type=MESH)
    own = pltpu.make_async_copy(dir_hbm, w_ref.at[c, 16 + me], own_sem)
    own.start()
    loads = [pltpu.make_async_copy(src, dst, in_sem.at[k]) for k, (src, dst) in enumerate((
        (hits_hbm, hits_ref), (noise_hbm, noise_ref), (st_hbm, st_ref), (tb_hbm, tb_ref)))]
    load_hits, load_noise, load_st, load_tb = loads
    loads += [pltpu.make_async_copy(src, map_ref.at[k], in_sem.at[4])
              for k, src in enumerate((sol_hbm, res_hbm, dir_hbm))]
    for copy in loads:
        copy.start()
    pl.semaphore_wait(barrier, len(greet))

    for k, dz in NEAR:
        remote(dir_hbm, w_ref.at[c, 16 * (1 - dz) + me], a_send, a_recv.at[3 * k + dz + 1], at(k, 0, dz)).start()
    for m in (2, 1, 3):
        remote(dir_hbm, w_ref.at[c, 16 + me], a_send, s2_recv.at[1], at(0, m, 0)).start()
    halo = []
    edge = 16384 - 512
    for k, (dev, off, slot) in enumerate(((partner, other * edge, c), (side, c * edge, other))):
        off = pl.multiple_of(off, 128)
        halo.append(remote(hits_hbm, hn_ref.at[slot], h_send.at[0], h_recv.at[0], dev))
        halo.append(remote(st_hbm.at[:, :, pl.ds(off, 512)], sh_ref.at[slot], h_send.at[1],
                           h_recv.at[1], dev))
    for copy in halo:
        copy.start()

    def relay(k, dz):
        shard = w_ref.at[c, 16 * (1 - dz) + 4 * b + lax.rem(a + 4 - k, 4)]
        remote(shard, shard, a_send, a_recv.at[3 * k + dz + 1], partner).wait_recv()
        for m in (2, 1, 3):
            remote(shard, shard, a_send, s2_recv.at[1 - dz], at(0, m, 0)).start()

    load_hits.wait()
    ids = halves(c)
    gather_side(hits_ref, oh_ref, ids)
    row_side(hits_ref, hrow_ref)
    bin_side(0, hrow_ref, oht_ref)
    for k, dz in RELAY[:3]:
        relay(k, dz)
    for k, dz in RELAY[3:]:
        relay(k, dz)
    bin_side(1, hrow_ref, oht_ref)
    load_noise.wait()
    weight_side(noise_ref, wt_ref)
    load_st.wait()
    own.wait()
    pltpu.make_async_copy(hn_ref, hn_ref, h_recv.at[0]).wait()
    pltpu.make_async_copy(sh_ref, sh_ref, h_recv.at[1]).wait()
    first = jnp.logical_and(ty == 0, c == 0)
    last = jnp.logical_and(ty == 3, c == 1)
    one_hot_rows(oh_ref, jnp.where(first, 768, hn_ref[0]), 124, 0, ids)
    one_hot_rows(oh_ref, jnp.where(last, 768, hn_ref[1]), 0, 33, ids)

    def swap(t):
        pltpu.make_async_copy(w_ref.at[c, 16 * t:16 * t + 12], w_ref.at[c, 16 * t:16 * t + 12], s2_recv.at[t]).wait()
        copy = remote(w_ref.at[c, 16 * t:16 * t + 16], w_ref.at[c, 16 * t:16 * t + 16], ap_send, ap_recv.at[t], partner)
        copy.start()

    def fill(t, core, base):
        if core is other:
            remote(w_ref.at[other, 16 * t:16 * t + 16], w_ref.at[other, 16 * t:16 * t + 16],
                   ap_send, ap_recv.at[t], partner).wait_recv()
        for p in range(0, 16, 2):
            for k in range(3):
                both = jnp.concatenate([w_ref[core, 16 * t + p, k], w_ref[core, 16 * t + p + 1, k]], 0)
                hi, lo = split(both if k == 0 else both * (1.0 / 2048.0))
                rows = slice(base + 8 * p, base + 8 * p + 16)
                tab_ref[rows, 128 * k:128 * k + 128] = hi
                tab_ref[rows, 384 + 128 * k:512 + 128 * k] = lo

    swap(1)
    fill(1, c, 0)
    fill(1, other, 128)
    scan_samples(0, 256, tab_ref, st_ref, sh_ref, oh_ref, x_ref)
    swap(0)
    swap(2)
    for dz in (2, 6):
        pl.semaphore_signal(hand_sem, inc=1, device_id=at(0, 0, dz), device_id_type=MESH)
    fill(0, c, 256)
    fill(2, c, 384)
    scan_samples(256, 512, tab_ref, st_ref, sh_ref, oh_ref, x_ref)
    fill(0, other, 512)
    fill(2, other, 640)
    scan_samples(512, 768, tab_ref, st_ref, sh_ref, oh_ref, x_ref)
    load_tb.wait()
    noise_filter(x_ref, tb_ref, wt_ref, st_ref, v_ref)

    out_pairs = []

    def give(k):
        out_pairs.append(remote(b_ref.at[0, k], pr_ref.at[k], cp_send, cp_recv.at[k], partner))
        out_pairs[k].start()

    def send_map(k):
        out_pairs[k].wait_recv()
        for p in range(4):
            rows = slice(96 * p, 96 * p + 96)
            s_ref[k, p] = b_ref[1, k, rows] + pr_ref[k, rows]
        for m in (2, 1, 3):
            remote(s_ref.at[k, lax.rem(b + m, 4)], q_ref.at[k, m - 1], q_send, q_recv.at[k], at(0, m, 0)).start()

    def pass_map(k):
        pltpu.make_async_copy(q_ref.at[k], q_ref.at[k], q_recv.at[k]).wait()
        for p in range(12):
            rows = slice(8 * p, 8 * p + 8)
            t_ref[p // 4, p % 4, k] = s_ref[k, b, rows] + q_ref[k, 0, rows] + q_ref[k, 1, rows] + q_ref[k, 2, rows]

    def pass_on():
        for t in (0, 2, 1):
            for n in (2, 1, 3, 0):
                src = t_ref.at[t, lax.rem(a + n, 4)]
                dst = r_ref.at[4 * t + a]
                if (n, t) == (0, 1):
                    pltpu.make_async_copy(src, dst, c_recv).start()
                else:
                    remote(src, dst, c_send, c_recv, at(n, 0, t - 1)).start()

    first_two = [bin_half(other, k, oht_ref, v_ref) for k in (0, 1)]
    for k in (0, 1):
        b_ref[0, k] = first_two[k]
    give(0)
    give(1)
    last, mine = bin_half(other, 2, oht_ref, v_ref), bin_half(c, 0, oht_ref, v_ref)
    b_ref[0, 2] = last
    b_ref[1, 0] = mine
    give(2)
    send_map(0)
    mine = [bin_half(c, k, oht_ref, v_ref) for k in (1, 2)]
    for k in (1, 2):
        b_ref[1, k] = mine[k - 1]
    send_map(1)
    send_map(2)
    pass_map(0)
    pass_map(1)
    pass_map(2)
    pass_on()
    pltpu.make_async_copy(map_ref, map_ref, in_sem.at[4]).wait()
    old = map_ref[1, 0] * map_ref[1, 0] + map_ref[1, 1] * map_ref[1, 1] + map_ref[1, 2] * map_ref[1, 2]
    old = jnp.sum(old, axis=0, keepdims=True)
    image = []
    parts = [jnp.zeros((8, 128), F32)] * 3
    pltpu.make_async_copy(r_ref, r_ref, c_recv).wait()
    for k in range(3):
        m = r_ref[0, k]
        for p in range(1, 12):
            m = m + r_ref[p, k]
        image.append(m)
        parts = [p + v for p, v in zip(parts, (map_ref[2, k] * m, map_ref[1, k] * m, m * m))]
    parts = [old] + [jnp.sum(p, axis=0, keepdims=True) for p in parts]
    part = lane_iota((1, 128)) // 32
    total = jnp.zeros((1, 128), F32)
    for k, p in enumerate(parts):
        p = p + pltpu.roll(p, 64, 1)
        p = p + pltpu.roll(p, 32, 1)
        total = jnp.where(part == k, p, total)
    n0_ref[...] = total
    cell = 8 * g + 2 * ty + c
    pltpu.make_async_copy(n0_ref, n1_ref.at[cell], n1_recv).start()
    for dx in (2, 1, 3, 0):
        for dy in (2, 1, 3, 0):
            for core in (other, c) if dx + dy else (other,):
                dev = (lax.rem(g + dx, 4), d, lax.rem(ty + dy, 4), core)
                remote(n0_ref, n1_ref.at[cell], n1_send, n1_recv, dev).start()
    pltpu.make_async_copy(n1_ref, n1_ref, n1_recv).wait()
    m1_ref[...] = jnp.sum(n1_ref[...], axis=0)
    pltpu.make_async_copy(m1_ref, n2_ref.at[d], n2_recv).start()
    pl.semaphore_wait(hand_sem, 2)
    for dz in (4, 3, 5, 2, 6, 1, 7):
        remote(m1_ref, n2_ref.at[d], n2_send, n2_recv, at(0, 0, dz)).start()
    pltpu.make_async_copy(hn_ref, hn_ref, h_send.at[0]).wait()
    pltpu.make_async_copy(sh_ref, sh_ref, h_send.at[1]).wait()
    pltpu.make_async_copy(w_ref.at[0], w_ref.at[0], ap_send).wait()
    pltpu.make_async_copy(pr_ref, pr_ref, cp_send).wait()
    pltpu.make_async_copy(w_ref.at[0, 0:47], w_ref.at[0, 0:47], a_send).wait()
    pltpu.make_async_copy(q_ref, q_ref, q_send).wait()
    pltpu.make_async_copy(r_ref.at[0:11], r_ref.at[0:11], c_send).wait()
    pltpu.make_async_copy(n2_ref, n2_ref, n2_recv).wait()
    sums = jnp.sum(n2_ref[...], axis=0)
    old_norm, curvature, cross_term, image_norm = (
        jnp.sum(jnp.where(part == k, sums, 0.0), axis=1, keepdims=True) for k in range(4))
    step = old_norm / curvature
    new_norm = old_norm - 2.0 * step * cross_term + step * step * image_norm
    ratio = new_norm / old_norm
    for k in range(3):
        dire = map_ref[2, k]
        out_ref[0, k] = map_ref[0, k] + step * dire
        nr = map_ref[1, k] - step * image[k]
        out_ref[1, k] = nr
        out_ref[2, k] = nr + ratio * dire
    pltpu.make_async_copy(n1_ref.at[0:31], n1_ref.at[0:31], n1_send).wait()
    pltpu.make_async_copy(n2_ref.at[0:7], n2_ref.at[0:7], n2_send).wait()


def step_kernel(sol, res, dire, hits, st, noise, tb):
    hbm = pl.BlockSpec(memory_space=pltpu.HBM)
    dma = pltpu.SemaphoreType.DMA
    scratch = [
        pltpu.VMEM((2, 48, 3, 8, 128), F32), pltpu.VMEM((768, 768), BF), pltpu.VMEM((4, 544, 768), BF),
        pltpu.VMEM((2, 384, 2048), BF), pltpu.VMEM((3, 16, 256), F32), pltpu.VMEM((544, 512), F32),
        pltpu.VMEM((2048, 768), BF), pltpu.VMEM((2, 3, 384, 128), F32),
        pltpu.VMEM((3, 384, 128), F32), pltpu.VMEM((3, 4, 96, 128), F32),
        pltpu.VMEM((3, 3, 96, 128), F32), pltpu.VMEM((3, 4, 3, 8, 128), F32), pltpu.VMEM((12, 3, 8, 128), F32),
        pltpu.VMEM((2, 16, 16384), jnp.int32), pltpu.VMEM((8, 512, 256), BF),
        pltpu.VMEM((2, 2, 16, 512), jnp.int32), pltpu.VMEM((2, 16, 128), jnp.int32),
        pltpu.VMEM((1, 128), F32), pltpu.VMEM((32, 1, 128), F32), pltpu.VMEM((1, 128), F32),
        pltpu.VMEM((8, 1, 128), F32), pltpu.VMEM((3, 3, 8, 128), F32), pltpu.VMEM((16, 128), jnp.int32), pltpu.VMEM((16, 512), F32),
        pltpu.VMEM((1, 2048), F32),
        dma((5,)), dma, dma, dma((12,)), dma((3,)), dma, dma((3,)), dma((2,)), dma((2,)),
        dma, dma((3,)), dma, dma, dma, dma((3,)), dma, dma, dma, dma,
        pltpu.SemaphoreType.REGULAR,
    ]
    return pl.pallas_call(
        kernel, out_shape=jax.ShapeDtypeStruct((3, 3, 8, 128), F32),
        in_specs=[hbm] * 7, out_specs=pl.BlockSpec(memory_space=pltpu.VMEM), scratch_shapes=scratch,
        compiler_params=pltpu.CompilerParams(
            vmem_limit_bytes=40 << 20, collective_id=0, has_side_effects=True),
    )(*(pltpu.with_memory_space_constraint(a, pltpu.HBM) for a in (sol, res, dire, hits, st, noise, tb)))


def shards(map_solution, map_residual, map_direction, hits, stokes_int, inv_noise):
    out = step_kernel(map_solution[:, 0], map_residual[:, 0], map_direction[:, 0], hits, stokes_int, inv_noise,
                      jnp.asarray(tables()))
    return (out[0][:, None], out[1][:, None], out[2][:, None])


def solution(mesh):
    torus = Mesh(
        mesh.devices.reshape(mesh.shape["group"], mesh.shape["det"], 4, 2),
        ("group", "det", "tm_0", "tm_1"),
    )
    TM = ("tm_0", "tm_1")
    tile = P(None, "det", ("group",) + TM, None)
    in_specs = (tile, tile, tile, P(("group", "det"), TM), P(None, ("group", "det"), TM), P(("group", "det"), None))
    return jax.shard_map(shards, mesh=torus, in_specs=in_specs, out_specs=(tile, tile, tile), check_vma=False)
```

```python
import math
import numpy as np
import jax, jax.numpy as jnp
from jax import lax
from jax.experimental import pallas as pl
from jax.experimental.pallas import tpu as pltpu
from jax.sharding import Mesh
from jax.sharding import PartitionSpec as P

BF = jnp.bfloat16
F32 = jnp.float32

def basis_tables():
    n = np.arange(256)[None, :]
    k = np.arange(256)[:, None]
    kk = np.where(k <= 128, k, k - 128)
    ang = 2 * np.pi * ((kk * n) % 256) / 256
    fe = np.where(k <= 128, np.cos(ang), np.sin(ang))
    fe = fe * np.where((k == 0) | (k == 128), math.sqrt(1 / 256), math.sqrt(2 / 256))
    kk = k % 128
    ang = 2 * np.pi * (((2 * kk + 1) * n) % 512) / 512
    fo = np.where(k < 128, np.cos(ang), np.sin(ang)) * math.sqrt(2 / 256)
    ang = 2 * np.pi * (((2 * k + 1) * n) % 1024) / 1024
    fc = np.cos(ang) / 16
    fs = np.sin(ang) / 16
    fs[:, 0] = np.where(np.arange(256) % 2 == 0, 1, -1) / 16
    return [fe, fo, fc, fs]

def split_np(a):
    a = np.asarray(a, np.float32)
    hi = a.astype(BF)
    lo = (a - hi.astype(np.float32)).astype(BF)
    return hi, lo

def tables():
    fe, fo, fc, fs = basis_tables()
    out = []
    for m in (fe.T, fo.T, fc.T, fs.T, fe * 0.5, fo * 0.5, fc, fs):
        hi, lo = split_np(m)
        out.append(np.concatenate([hi, lo], 0))
    return np.stack(out)

def split(x):
    hi = x.astype(BF)
    lo = (x - hi.astype(F32)).astype(BF)
    return hi, lo

def dot(a, b):
    return jnp.dot(a, b, preferred_element_type=F32)

def dot3(x, tab):
    hi, lo = split(x)
    th = tab[0:256, :]
    tl = tab[256:512, :]
    return dot(hi, th) + dot(hi, tl) + dot(lo, th)

def lane_iota(shape):
    return lax.broadcasted_iota(jnp.int32, shape, len(shape) - 1)

def take(x, idx):
    return jnp.take_along_axis(x, idx, axis=1)

def reverse256(a, b):
    lane = lane_iota(a.shape)
    p = lax.rem(128 - lane, 128)
    ap, bp = take(a, p), take(b, p)
    z = lane == 0
    return jnp.where(z, ap, bp), jnp.where(z, bp, ap)

def weight_tables(w):
    lane = lane_iota((16, 128))
    blk = [w[:, 128 * b:128 * b + 128] for b in range(4)]
    def pick(stride, off, blocks):
        per = 128 // stride
        idx = stride * lax.rem(lane, per) + off
        out = take(blk[blocks[0]], idx)
        for t, b in enumerate(blocks[1:], 1):
            out = jnp.where(lane // per == t, take(blk[b], idx), out)
        return out
    w0 = pick(4, 0, (0, 1, 2, 3))
    w2 = pick(4, 2, (0, 1, 2, 3))
    last = jnp.broadcast_to(w[:, 511:512], (16, 128))
    we = (w0, jnp.where(lane == 0, last, w0))
    wo = (w2, w2)
    wd = (pick(2, 1, (0, 1)), pick(2, 1, (2, 3)))
    return we, wo, wd

def hit_rows(hits):
    h = hits.astype(F32)
    a = jnp.floor(h * (1.0 / 256.0))
    b = h - 256.0 * a
    both = jnp.concatenate([a, b], 0).astype(BF)
    row = lax.broadcasted_iota(jnp.int32, (128, 2048), 0)
    col = lax.broadcasted_iota(jnp.int32, (128, 2048), 1)
    want = 4 * ((col // 16) % 32) + col // 512
    p = jnp.where(row == want, 1.0, 0.0).astype(BF)
    y = dot(both, p)
    y = 256.0 * y[:16] + y[16:]
    i = lax.broadcasted_iota(jnp.int32, (16, 2048), 0)
    c = lax.broadcasted_iota(jnp.int32, (16, 2048), 1)
    return jnp.sum(jnp.where(i == c % 16, y, 0.0), axis=0, keepdims=True)

def block_ids(tile, core):
    lane = lane_iota((16, 128))
    place, row = lane // 8, lax.rem(lane, 8)
    chip = (1 - core) * (4 * lax.rem(place, 4) + place // 4) + core * place
    return 256 * tile + 16 * chip + 8 * core + row


def halves(core):
    return [block_ids(t, k) for t, k in ((1, core), (1, 1 - core), (0, core), (2, core), (0, 1 - core), (2, 1 - core))]


def one_hot_rows(oh_ref, hits, cols, s, ids):
    for j in range(4):
        hb = jnp.broadcast_to(hits[:, cols + j:cols + j + 1], (16, 128))
        for k in range(6):
            oh_ref[j, 16 * s:16 * s + 16, 128 * k:128 * k + 128] = jnp.where(hb == ids[k], 1.0, 0.0).astype(BF)


def gather_side(hits_ref, oh_ref, ids):
    hits = hits_ref[...]
    for s in range(32):
        one_hot_rows(oh_ref, hits, 4 * s, s + 1, ids)


def row_side(hits_ref, hrow_ref):
    hits = hits_ref[...]
    hrow_ref[...] = hit_rows(hits)


def bin_side(core, hrow_ref, oht_ref):
    sub = lax.broadcasted_iota(jnp.int32, (16, 128), 0)
    pattern = (lax.rem(sub, 8) + (sub // 8) * (16 if core else 64) + 8 * core).astype(F32)

    def rows(t, carry):
        second, tile, first = t // 6, lax.rem(t, 6) // 2, 2 * lax.rem(t, 2)
        chip = 4 * second + first if core else 4 * first + second
        want = pattern + (256 * tile + 16 * chip).astype(F32)
        for k in range(16):
            hb = hrow_ref[:, 128 * k:128 * k + 128]
            oht_ref[core, pl.ds(pl.multiple_of(t * 16, 16), 16), 128 * k:128 * k + 128] = jnp.where(
                want == hb, 1.0, 0.0).astype(BF)
        return carry
    lax.fori_loop(0, 24, rows, 0)


def weight_side(noise_ref, wt_ref):
    we, wo, wd = weight_tables(noise_ref[...])
    for t, (a, b) in enumerate((we, wo, wd)):
        wt_ref[t, :, 0:128] = a
        wt_ref[t, :, 128:256] = b

def scan_samples(lo, hi, tab_ref, st_ref, sh_ref, oh_ref, x_ref):
    def one(j, carry):
        off = j * 128
        g = dot(oh_ref[j, :, lo:hi], tab_ref[lo:hi, :])
        gi = g[:, 0:128] + g[:, 384:512]
        gq = g[:, 128:256] + g[:, 512:640]
        gu = g[:, 256:384] + g[:, 640:768]
        for s in range(34):
            r = slice(16 * s, 16 * s + 16)
            if s == 0 or s == 33:
                e = 0 if s == 0 else 1
                q = sh_ref[e, 0, :, pl.ds(off, 128)]
                u = sh_ref[e, 1, :, pl.ds(off, 128)]
            else:
                o = off + 512 * (s - 1)
                q = st_ref[0, :, pl.ds(o, 128)]
                u = st_ref[1, :, pl.ds(o, 128)]
            q, u = q.astype(F32), u.astype(F32)
            v = gi[r] + q * gq[r] + u * gu[r]
            x_ref[r, pl.ds(off, 128)] = v if lo == 0 else x_ref[r, pl.ds(off, 128)] + v
        return carry
    for j in range(4):
        one(j, 0)

def noise_filter(x_ref, tb_ref, wt_ref, st_ref, v_ref):
    M = 256
    def chunk(t, carry):
        base = t * M
        def xs(c, d):
            return x_ref[pl.ds(base + 16 * d, M), 128 * c:128 * c + 128]
        u, v = [], []
        for c in range(4):
            y = 0.5 * (xs(c, 0) + xs(c, 2))
            x = xs(c, 1)
            u.append(x + y)
            v.append(x - y)
        ue = jnp.concatenate([u[0] + u[2], u[1] + u[3]], 1)
        uo = jnp.concatenate([u[0] - u[2], u[1] - u[3]], 1)
        r0, r1 = reverse256(v[2], v[3])
        z = lane_iota((M, 128)) == 0
        vc = jnp.concatenate([v[0] - jnp.where(z, 0.0, r0), v[1] - r1], 1)
        vs = jnp.concatenate([jnp.where(z, r0, v[0] + r0), v[1] + r1], 1)
        outs = []
        for t_, (a, wi) in enumerate(((ue, 0), (uo, 1), (vc, 2), (vs, 2))):
            c = dot3(a, tb_ref[t_])
            c = (c.reshape(M // 16, 16, 256) * wt_ref[wi][None]).reshape(M, 256)
            outs.append(dot3(c, tb_ref[4 + t_]))
        ae, ao, oc, os_ = outs
        oc0, oc1, os0, os1 = oc[:, :128], oc[:, 128:], os_[:, :128], os_[:, 128:]
        p0, p1 = jnp.where(z, os0, os0 - oc0), os1 - oc1
        d2, d3 = reverse256(p0, p1)
        d0, d1 = oc0 + jnp.where(z, 0.0, os0), oc1 + os1
        ae0, ae1, ao0, ao1 = ae[:, :128], ae[:, 128:], ao[:, :128], ao[:, 128:]
        for j, f in enumerate((ae0 + ao0 + d0, ae1 + ao1 + d1, ae0 - ao0 + d2, ae1 - ao1 + d3)):
            for i in range(M // 16):
                s = t * (M // 16) + i
                o = 128 * j + 512 * s
                q = st_ref[0, :, o:o + 128].astype(F32)
                w = st_ref[1, :, o:o + 128].astype(F32)
                r = 512 * j + 16 * s
                fi = f[16 * i:16 * i + 16]
                scaled = fi * (1.0 / 2048.0)
                for k, val in enumerate((fi, q * scaled, w * scaled)):
                    hi, lo = split(val)
                    v_ref[r:r + 16, 256 * k:256 * k + 128] = hi
                    v_ref[r:r + 16, 256 * k + 128:256 * k + 256] = lo
        return carry
    for t in range(512 // M):
        chunk(t, 0)


def bin_half(core, k, oht_ref, v_ref):
    g = dot(oht_ref[core], v_ref[:, 256 * k:256 * k + 256])
    return g[:, 0:128] + g[:, 128:256]


MESH = pl.DeviceIdType.MESH
NEAR = [(k, dz) for k in (2, 1, 3, 0) for dz in (1, -1, 0) if (k, dz) != (0, 0)]
RELAY = [(1, 0), (3, 0), (2, 0), (0, 1), (0, -1), (1, 1), (1, -1), (3, 1), (3, -1), (2, 1), (2, -1)]


def remote(src, dst, send, recv, where):
    return pltpu.make_async_remote_copy(
        src_ref=src, dst_ref=dst, send_sem=send, recv_sem=recv, device_id=where, device_id_type=MESH)


def kernel(sol_hbm, res_hbm, dir_hbm, hits_hbm, st_hbm, noise_hbm, tb_hbm, out_ref,
           w_ref, tab_ref, oh_ref, oht_ref, wt_ref, x_ref, v_ref, b_ref, pr_ref, s_ref, q_ref, t_ref, r_ref,
           st_ref, tb_ref, sh_ref, hn_ref, n0_ref, n1_ref, m1_ref, n2_ref, sol_ref, res_ref, dir_ref, hits_ref,
           noise_ref, hrow_ref, in_sem, own_sem, a_send, a_recv, s2_recv, ap_send, ap_recv, h_send, h_recv,
           q_send, q_recv, c_send, c_recv, cp_send, cp_recv, n1_send, n1_recv, n2_send, n2_recv, hand_sem):
    g, d, ty, c = (lax.axis_index(a) for a in ("group", "det", "tm_0", "tm_1"))
    other = 1 - c
    a = g * other + ty * c
    b = ty * other + g * c
    me = 4 * b + a
    partner = (g, d, ty, other)
    side = (g, d, lax.rem(ty + 3 + 2 * c, 4), other)

    def at(k, m, dz):
        pa, pb = lax.rem(a + k, 4), lax.rem(b + m, 4)
        return (pa * other + pb * c, lax.rem(d + dz + 8, 8), pb * other + pa * c, c)

    greet = [at(k, 0, dz) for k, dz in NEAR] + [at(0, m, 0) for m in (2, 1, 3)] + [side, partner]
    barrier = pltpu.get_barrier_semaphore()
    for dev in greet:
        pl.semaphore_signal(barrier, inc=1, device_id=dev, device_id_type=MESH)
    own = pltpu.make_async_copy(dir_hbm, w_ref.at[c, 16 + me], own_sem)
    own.start()
    loads = [pltpu.make_async_copy(src, dst, in_sem.at[k]) for k, (src, dst) in enumerate((
        (hits_hbm, hits_ref), (noise_hbm, noise_ref), (st_hbm, st_ref), (tb_hbm, tb_ref),
        (res_hbm, res_ref), (dir_hbm, dir_ref), (sol_hbm, sol_ref)))]
    for copy in loads:
        copy.start()
    load_hits, load_noise, load_st, load_tb, load_res, load_dir, load_sol = loads
    pl.semaphore_wait(barrier, len(greet))

    for k, dz in NEAR:
        remote(dir_hbm, w_ref.at[c, 16 * (1 - dz) + me], a_send, a_recv.at[3 * k + dz + 1], at(k, 0, dz)).start()
    for m in (2, 1, 3):
        remote(dir_hbm, w_ref.at[c, 16 + me], a_send, s2_recv.at[1], at(0, m, 0)).start()
    halo = []
    edge = 16384 - 512
    for k, (dev, off, slot) in enumerate(((partner, other * edge, c), (side, c * edge, other))):
        off = pl.multiple_of(off, 128)
        halo.append(remote(hits_hbm, hn_ref.at[slot], h_send.at[2 * k], h_recv.at[slot], dev))
        halo.append(remote(st_hbm.at[:, :, pl.ds(off, 512)], sh_ref.at[slot], h_send.at[2 * k + 1],
                           h_recv.at[2 + slot], dev))
    for copy in halo:
        copy.start()

    def relay(k, dz):
        shard = w_ref.at[c, 16 * (1 - dz) + 4 * b + lax.rem(a + 4 - k, 4)]
        remote(shard, shard, a_send, a_recv.at[3 * k + dz + 1], partner).wait_recv()
        for m in (2, 1, 3):
            remote(shard, shard, a_send, s2_recv.at[1 - dz], at(0, m, 0)).start()

    load_hits.wait()
    ids = halves(c)
    gather_side(hits_ref, oh_ref, ids)
    row_side(hits_ref, hrow_ref)
    bin_side(0, hrow_ref, oht_ref)
    for k, dz in RELAY[:3]:
        relay(k, dz)
    for k, dz in RELAY[3:]:
        relay(k, dz)
    bin_side(1, hrow_ref, oht_ref)
    load_noise.wait()
    weight_side(noise_ref, wt_ref)
    load_st.wait()
    own.wait()
    for k in range(2):
        remote(hits_hbm, hn_ref.at[k], h_send.at[0], h_recv.at[k], partner).wait_recv()
        remote(sh_ref.at[k], sh_ref.at[k], h_send.at[0], h_recv.at[2 + k], partner).wait_recv()
    first = jnp.logical_and(ty == 0, c == 0)
    last = jnp.logical_and(ty == 3, c == 1)
    one_hot_rows(oh_ref, jnp.where(first, 768, hn_ref[0]), 124, 0, ids)
    one_hot_rows(oh_ref, jnp.where(last, 768, hn_ref[1]), 0, 33, ids)

    pairs = []

    def swap(t):
        pltpu.make_async_copy(w_ref.at[c, 16 * t:16 * t + 12], w_ref.at[c, 16 * t:16 * t + 12], s2_recv.at[t]).wait()
        copy = remote(w_ref.at[c, 16 * t:16 * t + 16], w_ref.at[c, 16 * t:16 * t + 16], ap_send.at[t], ap_recv.at[t], partner)
        copy.start()
        pairs.append(copy)

    def fill(t, core, base):
        if core is other:
            remote(w_ref.at[other, 16 * t:16 * t + 16], w_ref.at[other, 16 * t:16 * t + 16],
                   ap_send.at[t], ap_recv.at[t], partner).wait_recv()
        for p in range(0, 16, 2):
            for k in range(3):
                both = jnp.concatenate([w_ref[core, 16 * t + p, k], w_ref[core, 16 * t + p + 1, k]], 0)
                hi, lo = split(both if k == 0 else both * (1.0 / 2048.0))
                rows = slice(base + 8 * p, base + 8 * p + 16)
                tab_ref[rows, 128 * k:128 * k + 128] = hi
                tab_ref[rows, 384 + 128 * k:512 + 128 * k] = lo

    swap(1)
    fill(1, c, 0)
    fill(1, other, 128)
    scan_samples(0, 256, tab_ref, st_ref, sh_ref, oh_ref, x_ref)
    swap(0)
    swap(2)
    for dz in (2, 6):
        pl.semaphore_signal(hand_sem, inc=1, device_id=at(0, 0, dz), device_id_type=MESH)
    fill(0, c, 256)
    fill(2, c, 384)
    scan_samples(256, 512, tab_ref, st_ref, sh_ref, oh_ref, x_ref)
    fill(0, other, 512)
    fill(2, other, 640)
    scan_samples(512, 768, tab_ref, st_ref, sh_ref, oh_ref, x_ref)
    load_tb.wait()
    noise_filter(x_ref, tb_ref, wt_ref, st_ref, v_ref)

    out_pairs = []

    def give(k):
        out_pairs.append(remote(b_ref.at[0, k], pr_ref.at[k], cp_send.at[k], cp_recv.at[k], partner))
        out_pairs[k].start()

    def send_map(k):
        out_pairs[k].wait_recv()
        for p in range(4):
            rows = slice(96 * p, 96 * p + 96)
            s_ref[k, p] = b_ref[1, k, rows] + pr_ref[k, rows]
        for m in (2, 1, 3):
            remote(s_ref.at[k, lax.rem(b + m, 4)], q_ref.at[k, m - 1], q_send, q_recv.at[k], at(0, m, 0)).start()

    def pass_map(k):
        pltpu.make_async_copy(q_ref.at[k], q_ref.at[k], q_recv.at[k]).wait()
        for p in range(12):
            rows = slice(8 * p, 8 * p + 8)
            t_ref[p // 4, p % 4, k] = s_ref[k, b, rows] + q_ref[k, 0, rows] + q_ref[k, 1, rows] + q_ref[k, 2, rows]

    def pass_on():
        for t in (0, 2, 1):
            for n in (2, 1, 3, 0):
                src = t_ref.at[t, lax.rem(a + n, 4)]
                dst = r_ref.at[4 * t + a]
                if (n, t) == (0, 1):
                    pltpu.make_async_copy(src, dst, c_recv).start()
                else:
                    remote(src, dst, c_send, c_recv, at(n, 0, t - 1)).start()

    first_two = [bin_half(other, k, oht_ref, v_ref) for k in (0, 1)]
    for k in (0, 1):
        b_ref[0, k] = first_two[k]
    give(0)
    give(1)
    last, mine = bin_half(other, 2, oht_ref, v_ref), bin_half(c, 0, oht_ref, v_ref)
    b_ref[0, 2] = last
    b_ref[1, 0] = mine
    give(2)
    send_map(0)
    mine = [bin_half(c, k, oht_ref, v_ref) for k in (1, 2)]
    for k in (1, 2):
        b_ref[1, k] = mine[k - 1]
    send_map(1)
    send_map(2)
    pass_map(0)
    pass_map(1)
    pass_map(2)
    pass_on()
    load_res.wait()
    load_dir.wait()
    load_sol.wait()
    image = []
    parts = [jnp.zeros((8, 128), F32)] * 4
    pltpu.make_async_copy(r_ref, r_ref, c_recv).wait()
    for k in range(3):
        m = r_ref[0, k]
        for p in range(1, 12):
            m = m + r_ref[p, k]
        image.append(m)
        res, dire = res_ref[k], dir_ref[k]
        parts = [p + v for p, v in zip(parts, (res * res, dire * m, res * m, m * m))]
    parts = [jnp.sum(p, axis=0, keepdims=True) for p in parts]
    part = lane_iota((1, 128)) // 32
    total = jnp.zeros((1, 128), F32)
    for k, p in enumerate(parts):
        p = p + pltpu.roll(p, 64, 1)
        p = p + pltpu.roll(p, 32, 1)
        total = jnp.where(part == k, p, total)
    n0_ref[...] = total
    cell = 8 * g + 2 * ty + c
    pltpu.make_async_copy(n0_ref, n1_ref.at[cell], n1_recv).start()
    for dx in (2, 1, 3, 0):
        for dy in (2, 1, 3, 0):
            for core in (other, c) if dx + dy else (other,):
                dev = (lax.rem(g + dx, 4), d, lax.rem(ty + dy, 4), core)
                remote(n0_ref, n1_ref.at[cell], n1_send, n1_recv, dev).start()
    pltpu.make_async_copy(n1_ref, n1_ref, n1_recv).wait()
    m1_ref[...] = jnp.sum(n1_ref[...], axis=0)
    pltpu.make_async_copy(m1_ref, n2_ref.at[d], n2_recv).start()
    pl.semaphore_wait(hand_sem, 2)
    for dz in (4, 3, 5, 2, 6, 1, 7):
        remote(m1_ref, n2_ref.at[d], n2_send, n2_recv, at(0, 0, dz)).start()
    for copy in halo + pairs + out_pairs:
        copy.wait_send()
    pltpu.make_async_copy(w_ref.at[0, 0:47], w_ref.at[0, 0:47], a_send).wait()
    pltpu.make_async_copy(q_ref, q_ref, q_send).wait()
    pltpu.make_async_copy(r_ref.at[0:11], r_ref.at[0:11], c_send).wait()
    pltpu.make_async_copy(n2_ref, n2_ref, n2_recv).wait()
    sums = jnp.sum(n2_ref[...], axis=0)
    old_norm, curvature, cross_term, image_norm = (
        jnp.sum(jnp.where(part == k, sums, 0.0), axis=1, keepdims=True) for k in range(4))
    step = old_norm / curvature
    new_norm = old_norm - 2.0 * step * cross_term + step * step * image_norm
    ratio = new_norm / old_norm
    for k in range(3):
        dire = dir_ref[k]
        out_ref[0, k] = sol_ref[k] + step * dire
        nr = res_ref[k] - step * image[k]
        out_ref[1, k] = nr
        out_ref[2, k] = nr + ratio * dire
    pltpu.make_async_copy(n1_ref.at[0:31], n1_ref.at[0:31], n1_send).wait()
    pltpu.make_async_copy(n2_ref.at[0:7], n2_ref.at[0:7], n2_send).wait()


def step_kernel(sol, res, dire, hits, st, noise, tb):
    hbm = pl.BlockSpec(memory_space=pltpu.HBM)
    dma = pltpu.SemaphoreType.DMA
    scratch = [
        pltpu.VMEM((2, 48, 3, 8, 128), F32), pltpu.VMEM((768, 768), BF), pltpu.VMEM((4, 544, 768), BF),
        pltpu.VMEM((2, 384, 2048), BF), pltpu.VMEM((3, 16, 256), F32), pltpu.VMEM((544, 512), F32),
        pltpu.VMEM((2048, 768), BF), pltpu.VMEM((2, 3, 384, 128), F32),
        pltpu.VMEM((3, 384, 128), F32), pltpu.VMEM((3, 4, 96, 128), F32),
        pltpu.VMEM((3, 3, 96, 128), F32), pltpu.VMEM((3, 4, 3, 8, 128), F32), pltpu.VMEM((12, 3, 8, 128), F32),
        pltpu.VMEM((2, 16, 16384), jnp.int32), pltpu.VMEM((8, 512, 256), BF),
        pltpu.VMEM((2, 2, 16, 512), jnp.int32), pltpu.VMEM((2, 16, 128), jnp.int32),
        pltpu.VMEM((1, 128), F32), pltpu.VMEM((32, 1, 128), F32), pltpu.VMEM((1, 128), F32),
        pltpu.VMEM((8, 1, 128), F32), pltpu.VMEM((3, 8, 128), F32), pltpu.VMEM((3, 8, 128), F32),
        pltpu.VMEM((3, 8, 128), F32), pltpu.VMEM((16, 128), jnp.int32), pltpu.VMEM((16, 512), F32),
        pltpu.VMEM((1, 2048), F32),
        dma((7,)), dma, dma, dma((12,)), dma((3,)), dma((3,)), dma((3,)), dma((4,)), dma((4,)),
        dma, dma((3,)), dma, dma, dma((3,)), dma((3,)), dma, dma, dma, dma,
        pltpu.SemaphoreType.REGULAR,
    ]
    return pl.pallas_call(
        kernel, out_shape=jax.ShapeDtypeStruct((3, 3, 8, 128), F32),
        in_specs=[hbm] * 7, out_specs=pl.BlockSpec(memory_space=pltpu.VMEM), scratch_shapes=scratch,
        compiler_params=pltpu.CompilerParams(
            vmem_limit_bytes=40 << 20, collective_id=0, has_side_effects=True),
    )(*(pltpu.with_memory_space_constraint(a, pltpu.HBM) for a in (sol, res, dire, hits, st, noise, tb)))


def shards(map_solution, map_residual, map_direction, hits, stokes_int, inv_noise):
    out = step_kernel(map_solution[:, 0], map_residual[:, 0], map_direction[:, 0], hits, stokes_int, inv_noise,
                      jnp.asarray(tables()))
    return (out[0][:, None], out[1][:, None], out[2][:, None])


def solution(mesh):
    torus = Mesh(
        mesh.devices.reshape(mesh.shape["group"], mesh.shape["det"], 4, 2),
        ("group", "det", "tm_0", "tm_1"),
    )
    TM = ("tm_0", "tm_1")
    tile = P(None, "det", ("group",) + TM, None)
    in_specs = (tile, tile, tile, P(("group", "det"), TM), P(None, ("group", "det"), TM), P(("group", "det"), None))
    return jax.shard_map(shards, mesh=torus, in_specs=in_specs, out_specs=(tile, tile, tile), check_vma=False)
```
